32 devices in a mesh: streams: 2 (over x), seq: 16 (over z, y, core).
Axes of the slice: x: 2, y: 2, z: 4, core: 2. Of those that a mesh axis runs over, the one named last changes fastest.
Arguments:
- queries: bfloat16 [8192, 2048], P(('streams', 'seq')), parts along dimension 0, may hold values from -13 to 13
- keyval: bfloat16 [2, 8192, 2048], P(None, ('streams', 'seq')), parts along dimension 1, may hold values from -13 to 13
Outputs:
- attended: bfloat16 [8192, 2048], P(('streams', 'seq')), parts along dimension 0
The draws below stay inside these ranges and needn't reach their ends.
There are 2 independent parts, one for each index of `streams`. The reference program is written for one: setup_inputs(seed, part) draws one part's arguments, and reference() takes and returns one part's arrays. A program takes and returns all parts, laid end to end along the dimension named above; each array names one. Nothing has to cross between parts.
All inputs are finite; a program needn't handle non-finite values.
Results may differ from the reference program's by a relative error of at most 0.0052.
Values may be sent and summed in bfloat16 or wider, within the bound.
No kernel may reach another device: no remote copies, remote signals or barrier semaphores. Data moves between devices by JAX's collectives and lax.ppermute only.
A program may use at most 128 MiB of HBM per device.

```python
import math
import jax
import jax.numpy as jnp
from jax import lax

HEADS = 16
HEAD_DIM = 128
BLOCK = 128
SEQ = 4096


def smooth_part(key):
    feature_count = HEADS * HEAD_DIM
    freq_key, phase_key, amp_key = jax.random.split(jax.random.fold_in(key, 17), 3)
    frequency = jax.random.randint(freq_key, (feature_count,), 1, 9).astype(jnp.float32)
    phases = jax.random.uniform(phase_key, (feature_count,), jnp.float32, -math.pi, math.pi)
    amplitude = jnp.exp(jax.random.uniform(amp_key, (feature_count,), jnp.float32, math.log(0.4), math.log(1.6)))
    position = jnp.arange(SEQ, dtype=jnp.float32) / SEQ
    return amplitude * jnp.sin(2.0 * math.pi * position[:, None] * frequency + phases)


def rough_part(key, salt, shape_here):
    return jnp.clip(jax.random.normal(jax.random.fold_in(key, salt), shape_here, jnp.float32), -4.0, 4.0)


def draw_queries(key, part):
    smooth = smooth_part(key)
    strength = 0.8
    return (rough_part(key, 1, smooth.shape) + strength * smooth).astype(jnp.bfloat16)


def draw_keyval(key, part):
    smooth = smooth_part(key)
    strength = 0.8
    key_rows = rough_part(key, 2, smooth.shape) + strength * smooth
    value_rows = rough_part(key, 3, smooth.shape) + 1.5 * smooth
    return jnp.stack((key_rows, value_rows)).astype(jnp.bfloat16)


def setup_inputs(seed: int = 0, part: int = 0) -> dict:
    keys = jax.random.split(jax.random.key(seed), 3)
    own_keys = jax.random.split(jax.random.fold_in(keys[2], part), 3)
    queries = draw_queries(jax.random.fold_in(jax.random.fold_in(keys[2], part), 71), part)
    keyval = draw_keyval(jax.random.fold_in(jax.random.fold_in(keys[2], part), 71), part)
    return dict(queries=queries, keyval=keyval)


neg_large = -1e+30
log_two = 0.6931471805599453

def halve_rows(pair_rows, along):
    old_shape = pair_rows.shape
    new_shape = old_shape[:along] + (old_shape[along] // 2, 2) + old_shape[along + 1:]
    widened = pair_rows.reshape(new_shape).astype(jnp.float32)
    pooled = (jnp.take(widened, 0, axis=along + 1) + jnp.take(widened, 1, axis=along + 1)) * 0.5
    return pooled.astype(jnp.bfloat16)

def attend(query_rows, key_rows, value_rows, key_bias, scaling):
    scores = jnp.einsum('gqhe,gkhe->ghqk', query_rows.astype(jnp.float32), key_rows.astype(jnp.float32)) * scaling
    if key_bias is not None:
        scores = scores + key_bias[:, None, None, :]
    row_max = lax.optimization_barrier(jnp.max(scores, axis=3))
    expons = jnp.exp(scores - row_max[..., None])
    row_sum = lax.optimization_barrier(jnp.sum(expons, axis=3))
    weighted = jnp.einsum('ghqk,gkhe->gqhe', expons.astype(jnp.bfloat16).astype(jnp.float32), value_rows.astype(jnp.float32))
    head_count = row_max.shape[1]
    return (jnp.transpose(row_max, (0, 2, 1)).reshape(-1, head_count), weighted.reshape(-1, head_count, weighted.shape[3]), jnp.transpose(row_sum, (0, 2, 1)).reshape(-1, head_count))

def combine(results, row_count):
    level_total = len(results)
    top_max, top_weighted, top_sum = results[level_total - 1]
    peak = top_max + (level_total - 1) * log_two
    numerator = top_weighted
    denominator = top_sum
    for level_index in range(level_total - 2, -1, -1):
        row_max, weighted, row_sum = results[level_index]
        ratio = row_max.shape[0] // peak.shape[0]
        peak = jnp.repeat(peak, ratio, axis=0)
        numerator = jnp.repeat(numerator, ratio, axis=0)
        denominator = jnp.repeat(denominator, ratio, axis=0)
        level_peak = row_max + level_index * log_two
        new_peak = jnp.maximum(peak, level_peak)
        carry_factor = jnp.exp(peak - new_peak)
        level_factor = jnp.exp(level_peak - new_peak)
        numerator = carry_factor[..., None] * numerator + level_factor[..., None] * weighted
        denominator = carry_factor * denominator + level_factor * row_sum
        peak = new_peak
    return (numerator / denominator[..., None]).astype(jnp.bfloat16)

def reference(queries, keyval):
    seq_len = queries.shape[0]
    feature_count = queries.shape[1]
    head_count = HEADS
    head_size = HEAD_DIM
    block_size = BLOCK
    scaling = 1.0 / math.sqrt(head_size)
    block_total = seq_len // block_size
    padded = jnp.pad(keyval, ((0, 0), (block_size, block_size), (0, 0)))
    slot_ids = jnp.arange(3 * block_size, dtype=jnp.int32) // block_size

    def fine_block(block_index):
        query_block = lax.dynamic_slice_in_dim(queries, block_index * block_size, block_size, 0)
        query_block = query_block.reshape(1, block_size, head_count, head_size)
        kv_block = lax.dynamic_slice_in_dim(padded, block_index * block_size, 3 * block_size, 1)
        kv_block = kv_block.reshape(2, 1, 3 * block_size, head_count, head_size)
        masked = (slot_ids == 0) & (block_index == 0) | (slot_ids == 2) & (block_index == block_total - 1)
        key_bias = jnp.where(masked, neg_large, 0.0).astype(jnp.float32)[None]
        return attend(query_block, kv_block[0], kv_block[1], key_bias, scaling)
    fine_out = lax.map(fine_block, jnp.arange(block_total, dtype=jnp.int32))
    results = [tuple((part_out.reshape((seq_len,) + part_out.shape[2:]) for part_out in fine_out))]
    top_level = block_total.bit_length() - 2
    level_q = queries
    level_kv = keyval
    for level_index in range(1, top_level + 1):
        level_q = halve_rows(level_q, 0)
        level_kv = halve_rows(level_kv, 1)
        level_rows = level_q.shape[0]
        group_total = level_rows // block_size

        def coarse_block(block_index, level_q=level_q, level_kv=level_kv):
            partner = jnp.bitwise_xor(block_index, 1).astype(jnp.int32)
            query_block = lax.dynamic_slice_in_dim(level_q, block_index * block_size, block_size, 0)
            query_block = query_block.reshape(1, block_size, head_count, head_size)
            kv_block = lax.dynamic_slice_in_dim(level_kv, partner * block_size, block_size, 1)
            kv_block = kv_block.reshape(2, 1, block_size, head_count, head_size)
            return attend(query_block, kv_block[0], kv_block[1], None, scaling)
        coarse_out = lax.map(coarse_block, jnp.arange(group_total, dtype=jnp.int32))
        results.append(tuple((part_out.reshape((level_rows,) + part_out.shape[2:]) for part_out in coarse_out)))
    return combine(results, seq_len).reshape(seq_len, feature_count)
```

```python
import functools
import math

import jax
import jax.numpy as jnp
from jax import lax
from jax.experimental import pallas as pl
from jax.experimental.pallas import tpu as pltpu
from jax.sharding import PartitionSpec as P

HEADS = 16
HEAD_DIM = 128
BLOCK = 128
GROUPS = 4
neg_large = -1e30
log_two = 0.6931471805599453
to_log2 = 1.0 / (math.sqrt(HEAD_DIM) * log_two)


def dot(left, right):
    return lax.dot_general(
        left, right, (((1,), (0,)), ((), ())), preferred_element_type=jnp.float32
    )


def dot_t(left, right):
    return lax.dot_general(
        left, right, (((1,), (1,)), ((), ())), preferred_element_type=jnp.float32
    )


def iota(shape, dim):
    return lax.broadcasted_iota(jnp.int32, shape, dim)


def halves(rows):
    shape = (rows // 2, rows)
    return jnp.where(iota(shape, 1) >> 1 == iota(shape, 0), 0.5, 0.0).astype(jnp.bfloat16)


def halve(rows):
    return dot(halves(rows.shape[0]), rows).astype(jnp.bfloat16)


def repeated_halve(rows, level):
    count = rows.shape[0]
    shape = (count, count)
    first = iota(shape, 0) >> level << level
    hit = (iota(shape, 1) == first) | (iota(shape, 1) == first + (1 << level - 1))
    return dot(jnp.where(hit, 0.5, 0.0).astype(jnp.bfloat16), rows).astype(jnp.bfloat16)


def pool_kernel(kv_ref, *out_refs):
    for which in range(2):
        rows = halve(kv_ref[which])
        for out_ref in out_refs:
            rows = halve(rows)
            out_ref[which] = rows


def pool(kv, first, count):
    rows = kv.shape[1]
    out_rows = [rows >> (first + step) for step in range(count)]
    return pl.pallas_call(
        pool_kernel if first == 2 else pool_once_kernel,
        grid=(2,),
        in_specs=[pl.BlockSpec((2, rows, kv.shape[2] // 2), lambda g: (0, 0, g))],
        out_specs=[
            pl.BlockSpec((2, out, kv.shape[2] // 2), lambda g: (0, 0, g)) for out in out_rows
        ],
        out_shape=[jax.ShapeDtypeStruct((2, out, kv.shape[2]), kv.dtype) for out in out_rows],
        name="pool",
    )(kv)


def pool_once_kernel(kv_ref, *out_refs):
    for which in range(2):
        rows = kv_ref[which]
        for out_ref in out_refs:
            rows = halve(rows)
            out_ref[which] = rows


def softmax_parts(queries, keys, values, state):
    exponents = []
    for query, (key, addend) in zip(queries, keys):
        exponent = dot_t(query, key) * to_log2
        if addend is not None:
            exponent = exponent + addend
        exponents.append(exponent)
    peak = functools.reduce(
        jnp.maximum, [jnp.max(exponent, axis=1, keepdims=True) for exponent in exponents]
    )
    if state is not None:
        old_peak, old_total, old_sum = state
        peak = jnp.maximum(peak, old_peak)
    expons = [jnp.exp2(exponent - peak) for exponent in exponents]
    total = functools.reduce(
        jnp.add, [jnp.sum(expon, axis=1, keepdims=True) for expon in expons]
    )
    weights = jnp.concatenate([expon.astype(jnp.bfloat16) for expon in expons], axis=1)
    weighted = dot(weights, jnp.concatenate(values, axis=0))
    if state is not None:
        factor = jnp.exp2(old_peak - peak)
        total = total + factor * old_total
        weighted = weighted + factor * old_sum
    return peak, total, weighted


def own_kernel(pos_ref, q_ref, kv_ref, sum_ref, stat_ref, edge_ref):
    per_group = q_ref.shape[1] // HEAD_DIM
    rows = q_ref.shape[0]
    lane = iota((rows, 128), 1)
    stats = jnp.zeros((rows, 128), jnp.float32)
    for head in range(per_group):
        cols = pl.ds(head * HEAD_DIM, HEAD_DIM)
        peak, total, weighted = softmax_parts(
            [q_ref[:, cols]], [(kv_ref[0, :, cols], None)], [kv_ref[1, :, cols]], None
        )
        sum_ref[:, cols] = weighted
        stats = jnp.where(lane == head, peak, stats)
        stats = jnp.where(lane == head + 64, total, stats)
    stat_ref[0] = stats
    outer = pl.ds(pl.multiple_of(pos_ref[0] * BLOCK, BLOCK), BLOCK)
    edge_ref[...] = kv_ref[:, outer, :]


def near_kernel(
    pos_ref, q_ref, inner_ref, mine_ref, theirs_ref, sum_ref, stat_ref, *out_refs
):
    new_sum_ref, new_stat_ref = out_refs[:2]
    up_refs = out_refs[2:]
    per_group = q_ref.shape[1] // HEAD_DIM
    rows = q_ref.shape[0]
    core = pos_ref[0]
    up = q_ref[...]
    ups = []
    for level in range(1, 3 + len(up_refs)):
        up = repeated_halve(up, level)
        ups.append(up)
    for up_ref, up in zip(up_refs, ups[2:]):
        up_ref[...] = up
    level_keys = halve(inner_ref[0])
    level_values = halve(inner_ref[1])
    lane = iota((BLOCK, 128), 1)
    up_1 = ups[0]
    up_2 = ups[1]
    inner_rows = pl.ds(pl.multiple_of(core * BLOCK, BLOCK), BLOCK)
    for block in range(2):
        span = slice(block * BLOCK, (block + 1) * BLOCK)
        stats = jnp.zeros((BLOCK, 128), jnp.float32)
        bias = jnp.where(core == 1 - block, 0.0, neg_large)
        for head in range(per_group):
            cols = slice(head * HEAD_DIM, (head + 1) * HEAD_DIM)
            state = (
                stat_ref[0, span, head : head + 1],
                stat_ref[0, span, head + 64 : head + 65],
                sum_ref[span, cols],
            )
            peak, total, weighted = softmax_parts(
                [q_ref[span, cols], up_1[span, cols], up_2[span, cols]],
                [
                    (inner_ref[0, inner_rows, cols], bias),
                    (level_keys[:, cols], 1.0),
                    (jnp.concatenate([mine_ref[0, :, cols], theirs_ref[0, :, cols]], 0), 2.0),
                ],
                [
                    inner_ref[1, inner_rows, cols],
                    level_values[:, cols],
                    mine_ref[1, :, cols],
                    theirs_ref[1, :, cols],
                ],
                state,
            )
            new_sum_ref[span, cols] = weighted
            stats = jnp.where(lane == head, peak, stats)
            stats = jnp.where(lane == head + 64, total, stats)
        new_stat_ref[0, span, :] = stats


def far_kernel(levels, pos_ref, q_ref, edge_ref, mine_ref, theirs_ref, sum_ref, stat_ref, *refs):
    out_ref = refs[-1]
    up_refs = refs[:levels]
    more_refs = refs[levels:-1]
    per_group = q_ref.shape[1] // HEAD_DIM
    core = pos_ref[0]
    for block in range(2):
        span = slice(block * BLOCK, (block + 1) * BLOCK)
        bias = jnp.where((core == block) & (pos_ref[1] == 1), 0.0, neg_large)
        for head in range(per_group):
            cols = slice(head * HEAD_DIM, (head + 1) * HEAD_DIM)
            state = (
                stat_ref[0, span, head : head + 1],
                stat_ref[0, span, head + 64 : head + 65],
                sum_ref[span, cols],
            )
            queries = [q_ref[span, cols]] + [up_ref[span, cols] for up_ref in up_refs]
            keys = [(edge_ref[0, :, cols], bias)]
            values = [edge_ref[1, :, cols]]
            for level in range(2):
                part = slice(level * 64, (level + 1) * 64)
                keys.append(
                    (
                        jnp.concatenate(
                            [mine_ref[0, part, cols], theirs_ref[0, part, cols]], 0
                        ),
                        level + 3.0,
                    )
                )
                values += [mine_ref[1, part, cols], theirs_ref[1, part, cols]]
            for level, more_ref in enumerate(more_refs):
                keys.append((more_ref[0, :, cols], level + 5.0))
                values.append(more_ref[1, :, cols])
            _, total, weighted = softmax_parts(queries, keys, values, state)
            out_ref[span, cols] = (weighted / total).astype(out_ref.dtype)


def specs(arrays, width):
    out = []
    for array in arrays:
        if array.ndim == 2:
            out.append(pl.BlockSpec((array.shape[0], width), lambda g, pos: (0, g)))
        elif array.shape[2] == 128:
            out.append(pl.BlockSpec((1,) + array.shape[1:], lambda g, pos: (g, 0, 0)))
        else:
            out.append(pl.BlockSpec(array.shape[:2] + (width,), lambda g, pos: (0, 0, g)))
    return out


def grouped(kernel, position, inputs, outputs, name, flops):
    width = inputs[0].shape[1] // GROUPS
    return pl.pallas_call(
        kernel,
        grid_spec=pltpu.PrefetchScalarGridSpec(
            num_scalar_prefetch=1,
            grid=(GROUPS,),
            in_specs=specs(inputs, width),
            out_specs=specs(outputs, width),
        ),
        out_shape=outputs,
        cost_estimate=pl.CostEstimate(
            flops=flops, bytes_accessed=8 << 20, transcendentals=1 << 20
        ),
        name=name,
    )(position, *inputs)


def sent(array, stride):
    count = lax.axis_size("seq")
    return lax.ppermute(array, "seq", [(i, i ^ stride) for i in range(count)])


def halve_rows(pairs):
    wide = pairs.reshape(2, pairs.shape[1] // 2, 2, pairs.shape[2]).astype(jnp.float32)
    return ((wide[:, :, 0] + wide[:, :, 1]) * 0.5).astype(jnp.bfloat16)


def on_device(queries, keyval):
    count = lax.axis_size("seq")
    levels = count.bit_length() - 1
    index = lax.axis_index("seq")
    core = index % 2
    inside = jnp.where(core == 0, index > 0, index < count - 1)
    position = jnp.stack((core, inside.astype(core.dtype)))
    rows, features = queries.shape
    sums = jax.ShapeDtypeStruct((rows, features), jnp.float32)
    stats = jax.ShapeDtypeStruct((GROUPS, rows, 128), jnp.float32)
    like_q = jax.ShapeDtypeStruct(queries.shape, queries.dtype)

    own_2, own_3, own_4 = pool(keyval, 2, 3)
    side_2 = sent(own_2, 2)
    far_4 = sent(own_4, 8)
    far_4x = sent(own_4, 12)
    far_3 = sent(own_3, 4)
    inner = sent(keyval, 1)
    sum_0, stat_0, edge = grouped(
        own_kernel,
        position,
        [queries, keyval],
        [sums, stats, jax.ShapeDtypeStruct((2, BLOCK, features), keyval.dtype)],
        "own",
        2 << 30,
    )
    links = [(i, i + 1) for i in range(1, count - 1, 2)]
    edge = lax.ppermute(edge, "seq", links + [(j, i) for i, j in links])
    side_3, side_4 = pool(side_2, 1, 2)
    late_3 = sent(side_3, 4)
    late_4 = sent(side_4, 8)
    late_4x = sent(side_4, 12)
    other_2 = sent(side_2, 1)
    sum_1, stat_1, *ups = grouped(
        near_kernel,
        position,
        [queries, inner, side_2, other_2, sum_0, stat_0],
        [sums, stats] + [like_q] * (levels - 2),
        "near",
        2 << 30,
    )
    mine = jnp.concatenate((far_3, late_3, far_4, far_4x, late_4, late_4x), axis=1)
    theirs = sent(mine, 1)
    more = []
    if levels > 4:
        own = halve_rows(halve_rows(jnp.concatenate((keyval, inner), axis=1)))
        own = halve_rows(jnp.concatenate((own, side_2, other_2), axis=1))
        own = jnp.concatenate((own, mine[:, :64], theirs[:, :64]), axis=1)
        own = jnp.concatenate((halve_rows(own), mine[:, 64:], theirs[:, 64:]), axis=1)
        own = halve_rows(own)
        for level in range(5, levels + 1):
            more.append(sent(own, 1 << level - 1))
            own = halve_rows(jnp.concatenate((own, more[-1]), axis=1))
    return grouped(
        functools.partial(far_kernel, levels - 2),
        position,
        [queries, edge, mine, theirs, sum_1, stat_1] + ups + more,
        [like_q],
        "far",
        2 << 30,
    )[0]


def solution(mesh):
    return jax.shard_map(
        on_device,
        mesh=mesh,
        in_specs=(P(("streams", "seq"), None), P(None, ("streams", "seq"), None)),
        out_specs=P(("streams", "seq"), None),
        check_vma=False,
    )
```

```python
import functools
import math

import jax
import jax.numpy as jnp
from jax import lax
from jax.experimental import pallas as pl
from jax.experimental.pallas import tpu as pltpu
from jax.sharding import PartitionSpec as P

HEADS = 16
HEAD_DIM = 128
BLOCK = 128
neg_large = -1e30
log_two = 0.6931471805599453
to_log2 = 1.0 / (math.sqrt(HEAD_DIM) * log_two)
VMEM = pl.BlockSpec(memory_space=pltpu.VMEM)
ANY = pl.BlockSpec(memory_space=pl.ANY)
SMEM = pl.BlockSpec(memory_space=pltpu.SMEM)


def dot(left, right):
    return lax.dot_general(
        left, right, (((1,), (0,)), ((), ())), preferred_element_type=jnp.float32
    )


def dot_t(left, right):
    return lax.dot_general(
        left, right, (((1,), (1,)), ((), ())), preferred_element_type=jnp.float32
    )


def iota(shape, dim):
    return lax.broadcasted_iota(jnp.int32, shape, dim)


def halve(rows):
    shape = (rows.shape[0] // 2, rows.shape[0])
    pairs = jnp.where(iota(shape, 1) >> 1 == iota(shape, 0), 0.5, 0.0).astype(jnp.bfloat16)
    return dot(pairs, rows).astype(jnp.bfloat16)


def repeated_halve(rows, level):
    count = rows.shape[0]
    shape = (count, count)
    first = iota(shape, 0) >> level << level
    hit = (iota(shape, 1) == first) | (iota(shape, 1) == first + (1 << level - 1))
    return dot(jnp.where(hit, 0.5, 0.0).astype(jnp.bfloat16), rows).astype(jnp.bfloat16)


def with_ones(values):
    return jnp.concatenate([values, jnp.ones(values.shape, values.dtype)], axis=1)


def row_max(scores):
    return jnp.max(scores, axis=1, keepdims=True)


def own_pool_kernel(kv_ref, *out_refs):
    for which in range(2):
        rows = halve(kv_ref[which])
        for out_ref in out_refs:
            rows = halve(rows)
            out_ref[which] = rows


def side_pool_kernel(after_ref, kv_ref, *out_refs):
    for which in range(2):
        rows = kv_ref[which]
        for out_ref in out_refs:
            rows = halve(rows)
            out_ref[which] = rows


def join_kernel(after_ref, *refs):
    start = 0
    for ref in refs[:-1]:
        refs[-1][:, start : start + ref.shape[1], :] = ref[...]
        start += ref.shape[1]


def own_kernel(core_ref, q_ref, kv_ref, mean_ref, log_ref, edge_ref):
    outer = pl.ds(pl.multiple_of(core_ref[0] * BLOCK, BLOCK), BLOCK)
    edge_ref[...] = kv_ref[:, outer, :]
    for head in range(HEADS):
        cols = slice(head * HEAD_DIM, (head + 1) * HEAD_DIM)
        scores = dot_t(q_ref[:, cols], kv_ref[0, :, cols])
        peak = row_max(scores) * to_log2
        weights = jnp.exp2(scores * to_log2 - peak).astype(jnp.bfloat16)
        both = dot(weights, with_ones(kv_ref[1, :, cols]))
        total = both[:, HEAD_DIM:]
        mean_ref[:, cols] = both[:, :HEAD_DIM] / total
        log_ref[:, cols] = jnp.log2(total) + peak


def spans(core):
    edge = pl.ds(pl.multiple_of(core * BLOCK, BLOCK), BLOCK)
    other = pl.ds(pl.multiple_of((1 - core) * BLOCK, BLOCK), BLOCK)
    return edge, other


def attend(first, second, cols, fine, bias, coarse, mean_ref, log_ref):
    def rows(ref):
        return jnp.concatenate([ref[first, cols], ref[second, cols]], axis=0)

    query_ref, key, value = fine
    near = dot_t(query_ref[first, cols], key)
    if bias is not None:
        near = near + bias
    scores = [dot_t(rows(query_ref), jnp.concatenate(keys, 0)) for query_ref, keys, _, _ in coarse]
    peak = functools.reduce(jnp.maximum, [row_max(score) for score in scores])
    peak = jnp.concatenate([jnp.maximum(peak[:BLOCK], row_max(near)), peak[BLOCK:]], axis=0)
    logs = rows(log_ref)
    peak = jnp.maximum(peak * to_log2, logs)
    weights = [
        jnp.exp2(score * to_log2 - (peak - level)).astype(jnp.bfloat16)
        for score, (_, _, _, level) in zip(scores, coarse)
    ]
    values = [value for _, _, parts, _ in coarse for value in parts]
    both = dot(jnp.concatenate(weights, axis=1), with_ones(jnp.concatenate(values, axis=0)))
    weights = jnp.exp2(near * to_log2 - peak[:BLOCK]).astype(jnp.bfloat16)
    near = dot(weights, with_ones(value))
    both = jnp.concatenate([both[:BLOCK] + near, both[BLOCK:]], axis=0)
    factor = jnp.exp2(logs - peak)
    total = both[:, HEAD_DIM:] + factor
    mean = (both[:, :HEAD_DIM] + factor * rows(mean_ref)) / total
    return mean, total, peak


def near_kernel(core_ref, q_ref, inner_ref, mine_ref, theirs_ref, mean_ref, log_ref, *refs):
    new_mean_ref, new_log_ref, *up_refs = refs[:-4]
    up_1_ref, up_2_ref, keys_ref, values_ref = refs[-4:]
    core = core_ref[0]
    edge, other = spans(core)
    up = q_ref[...]
    for level, ref in enumerate([up_1_ref, up_2_ref] + up_refs, 1):
        up = repeated_halve(up, level)
        ref[...] = up
    keys_ref[...] = halve(inner_ref[0])
    values_ref[...] = halve(inner_ref[1])
    for head in range(HEADS):
        cols = slice(head * HEAD_DIM, (head + 1) * HEAD_DIM)
        mean, total, peak = attend(
            other,
            edge,
            cols,
            (q_ref, inner_ref[0, edge, cols], inner_ref[1, edge, cols]),
            None,
            [
                (up_1_ref, [keys_ref[:, cols]], [values_ref[:, cols]], 1.0),
                (
                    up_2_ref,
                    [mine_ref[0, :, cols], theirs_ref[0, :64, cols]],
                    [mine_ref[1, :, cols], theirs_ref[1, :64, cols]],
                    2.0,
                ),
            ],
            mean_ref,
            log_ref,
        )
        logs = jnp.log2(total) + peak
        new_mean_ref[other, cols] = mean[:BLOCK]
        new_mean_ref[edge, cols] = mean[BLOCK:]
        new_log_ref[other, cols] = logs[:BLOCK]
        new_log_ref[edge, cols] = logs[BLOCK:]


def far_kernel(core_ref, q_ref, edge_ref, early_ref, their_early_ref, late_ref, their_late_ref, mean_ref, log_ref, *refs):
    out_ref = refs[-1]
    count = len(refs) // 2 + 1
    up_refs = refs[:count]
    more_refs = refs[count:-1]
    core = core_ref[0]
    edge, other = spans(core)
    bias = jnp.where(core_ref[1] == 1, 0.0, neg_large)
    for head in range(HEADS):
        cols = slice(head * HEAD_DIM, (head + 1) * HEAD_DIM)

        def parts(which, level):
            early = slice(0, 32) if level == 3 else slice(32, 64)
            theirs = slice(64, 96) if level == 3 else slice(96, 128)
            return [
                early_ref[which, early, cols],
                late_ref[which, early, cols],
                their_early_ref[which, theirs, cols],
                their_late_ref[which, early, cols],
            ]

        coarse = [
            (up_refs[level - 3], parts(0, level), parts(1, level), float(level))
            for level in (3, 4)
        ]
        for level, more_ref in enumerate(more_refs, 5):
            coarse.append(
                (up_refs[level - 3], [more_ref[0, :, cols]], [more_ref[1, :, cols]], float(level))
            )
        mean, _, _ = attend(
            edge,
            other,
            cols,
            (q_ref, edge_ref[0, :, cols], edge_ref[1, :, cols]),
            bias,
            coarse,
            mean_ref,
            log_ref,
        )
        mean = mean.astype(out_ref.dtype)
        out_ref[edge, cols] = mean[:BLOCK]
        out_ref[other, cols] = mean[BLOCK:]


def call(kernel, in_specs, outputs, name, micros, *inputs, scratch=()):
    return pl.pallas_call(
        kernel,
        in_specs=in_specs,
        out_specs=[VMEM] * len(outputs),
        out_shape=[jax.ShapeDtypeStruct(shape, dtype) for shape, dtype in outputs],
        scratch_shapes=[pltpu.VMEM(shape, dtype) for shape, dtype in scratch],
        cost_estimate=pl.CostEstimate(
            flops=micros * 1_000_000_000, bytes_accessed=1 << 20, transcendentals=0
        ),
        compiler_params=pltpu.CompilerParams(vmem_limit_bytes=16 << 20),
        name=name,
    )(*inputs)


def sent(array, stride):
    count = lax.axis_size("seq")
    return lax.ppermute(array, "seq", [(i, i ^ stride) for i in range(count)])


def halve_rows(pairs):
    wide = pairs.reshape(2, pairs.shape[1] // 2, 2, pairs.shape[2]).astype(jnp.float32)
    return ((wide[:, :, 0] + wide[:, :, 1]) * 0.5).astype(jnp.bfloat16)


def on_device(queries, keyval):
    count = lax.axis_size("seq")
    levels = count.bit_length() - 1
    index = lax.axis_index("seq")
    core = index % 2
    inside = jnp.where(core == 0, index > 0, index < count - 1)
    position = jnp.stack((core, inside.astype(core.dtype)))
    rows, features = queries.shape
    narrow = keyval.dtype
    wide = ((rows, features), jnp.float32)
    up = ((rows, features), narrow)

    def some(count):
        return ((2, count, features), narrow)

    own_2, own_3, own_4 = call(
        own_pool_kernel, [VMEM], [some(64), some(32), some(16)], "pool", 1, keyval
    )
    side_2 = sent(own_2, 2)
    inner = sent(keyval, 1)
    early = [sent(own_3, 4), sent(own_4, 8), sent(own_4, 12)]
    mean, log, edge = call(
        own_kernel,
        [SMEM, VMEM, VMEM],
        [wide, wide, some(BLOCK)],
        "own",
        4,
        position,
        queries,
        keyval,
    )
    links = [(i, i + 1) for i in range(1, count - 1, 2)]
    edge = lax.ppermute(edge, "seq", links + [(j, i) for i, j in links])
    side_3, side_4 = call(
        side_pool_kernel, [ANY, VMEM], [some(32), some(16)], "side", 1, log, side_2
    )
    late = [sent(side_3, 4), sent(side_4, 8), sent(side_4, 12)]
    (early,) = call(
        join_kernel, [ANY] + [VMEM] * 3, [some(64)], "early", 1, side_3, *early
    )
    theirs = sent(jnp.concatenate((side_2, early), axis=1), 1)
    mean, log, *ups = call(
        near_kernel,
        [SMEM] + [VMEM] * 6,
        [wide, wide] + [up] * (levels - 2),
        "near",
        4,
        position,
        queries,
        inner,
        side_2,
        theirs,
        mean,
        log,
        scratch=[up, up, ((BLOCK, features), narrow), ((BLOCK, features), narrow)],
    )
    (late,) = call(join_kernel, [ANY] + [VMEM] * 3, [some(64)], "late", 1, log, *late)
    their_late = sent(late, 1)
    more = []
    if levels > 4:
        own = halve_rows(halve_rows(jnp.concatenate((keyval, inner), axis=1)))
        own = halve_rows(jnp.concatenate((own, side_2, theirs[:, :64]), axis=1))
        quarters = (early, late, theirs[:, 64:], their_late)
        own = [own] + [quarter[:, :32] for quarter in quarters]
        own = [halve_rows(jnp.concatenate(own, axis=1))]
        own = halve_rows(jnp.concatenate(own + [part[:, 32:] for part in quarters], axis=1))
        for level in range(5, levels + 1):
            more.append(sent(own, 1 << level - 1))
            own = halve_rows(jnp.concatenate((own, more[-1]), axis=1))
    far = [position, queries, edge, early, theirs, late, their_late, mean, log] + ups + more
    return call(far_kernel, [SMEM] + [VMEM] * (len(far) - 1), [up], "far", 4, *far)[0]


def solution(mesh):
    return jax.shard_map(
        on_device,
        mesh=mesh,
        in_specs=(P(("streams", "seq"), None), P(None, ("streams", "seq"), None)),
        out_specs=P(("streams", "seq"), None),
        check_vma=False,
    )
```

```python
import functools
import math

import jax
import jax.numpy as jnp
from jax import lax
from jax.experimental import pallas as pl
from jax.experimental.pallas import tpu as pltpu
from jax.sharding import PartitionSpec as P

HEADS = 16
HEAD_DIM = 128
BLOCK = 128
neg_large = -1e30
log_two = 0.6931471805599453
to_log2 = 1.0 / (math.sqrt(HEAD_DIM) * log_two)
VMEM = pl.BlockSpec(memory_space=pltpu.VMEM)
ANY = pl.BlockSpec(memory_space=pl.ANY)
SMEM = pl.BlockSpec(memory_space=pltpu.SMEM)


def dot(left, right):
    return lax.dot_general(
        left, right, (((1,), (0,)), ((), ())), preferred_element_type=jnp.float32
    )


def dot_t(left, right):
    return lax.dot_general(
        left, right, (((1,), (1,)), ((), ())), preferred_element_type=jnp.float32
    )


def iota(shape, dim):
    return lax.broadcasted_iota(jnp.int32, shape, dim)


def halve(rows):
    shape = (rows.shape[0] // 2, rows.shape[0])
    pairs = jnp.where(iota(shape, 1) >> 1 == iota(shape, 0), 0.5, 0.0).astype(jnp.bfloat16)
    return dot(pairs, rows).astype(jnp.bfloat16)


def repeated_halve(rows, level):
    count = rows.shape[0]
    shape = (count, count)
    first = iota(shape, 0) >> level << level
    hit = (iota(shape, 1) == first) | (iota(shape, 1) == first + (1 << level - 1))
    return dot(jnp.where(hit, 0.5, 0.0).astype(jnp.bfloat16), rows).astype(jnp.bfloat16)


def with_ones(values):
    return jnp.concatenate([values, jnp.ones(values.shape, values.dtype)], axis=1)


def row_max(scores):
    return jnp.max(scores, axis=1, keepdims=True)


def own_pool_kernel(core_ref, kv_ref, edge_ref, *out_refs):
    outer = pl.ds(pl.multiple_of(core_ref[0] * BLOCK, BLOCK), BLOCK)
    edge_ref[...] = kv_ref[:, outer, :]
    for which in range(2):
        rows = halve(kv_ref[which])
        for out_ref in out_refs:
            rows = halve(rows)
            out_ref[which] = rows


def side_pool_kernel(*refs):
    kv_ref, _, *out_refs = refs[-4:]
    for which in range(2):
        rows = kv_ref[which]
        for out_ref in out_refs:
            rows = halve(rows)
            out_ref[which] = rows


def join_kernel(after_1, after_2, *refs):
    start = 0
    for ref in refs[:-1]:
        refs[-1][:, start : start + ref.shape[1], :] = ref[...]
        start += ref.shape[1]


def ups_kernel(after_ref, q_ref, *refs):
    up = q_ref[...]
    for level, ref in enumerate(refs, 1):
        up = repeated_halve(up, level)
        ref[...] = up


def own_kernel(after_ref, q_ref, kv_ref, mean_ref, log_ref):
    for head in range(HEADS):
        cols = slice(head * HEAD_DIM, (head + 1) * HEAD_DIM)
        scores = dot_t(q_ref[:, cols], kv_ref[0, :, cols])
        peak = row_max(scores) * to_log2
        weights = jnp.exp2(scores * to_log2 - peak).astype(jnp.bfloat16)
        both = dot(weights, with_ones(kv_ref[1, :, cols]))
        total = both[:, HEAD_DIM:]
        mean_ref[:, cols] = both[:, :HEAD_DIM] / total
        log_ref[:, cols] = jnp.log2(total) + peak


def by_core(core_ref, body):
    blocks = slice(0, BLOCK), slice(BLOCK, 2 * BLOCK)

    @pl.when(core_ref[0] == 0)
    def _():
        body(*blocks)

    @pl.when(core_ref[0] == 1)
    def _():
        body(*blocks[::-1])


def attend(first, second, cols, fine, bias, coarse, mean_ref, log_ref):
    def rows(ref):
        return jnp.concatenate([ref[first, cols], ref[second, cols]], axis=0)

    query_ref, key, value = fine
    near = dot_t(query_ref[first, cols], key)
    if bias is not None:
        near = near + bias
    scores = [dot_t(rows(level[0]), level[1]) for level in coarse]
    peak = functools.reduce(jnp.maximum, scores)
    peak = jnp.concatenate([jnp.maximum(peak[:BLOCK], near), peak[BLOCK:]], axis=0)
    logs = rows(log_ref)
    peak = jnp.maximum(row_max(peak) * to_log2, logs)
    weights = [
        jnp.exp2(score * to_log2 - (peak - level)).astype(jnp.bfloat16)
        for score, (_, _, _, level) in zip(scores, coarse)
    ]
    values = jnp.concatenate([level[2] for level in coarse], axis=0)
    both = dot(jnp.concatenate(weights, axis=1), with_ones(values))
    weights = jnp.exp2(near * to_log2 - peak[:BLOCK]).astype(jnp.bfloat16)
    near = dot(weights, with_ones(value))
    both = jnp.concatenate([both[:BLOCK] + near, both[BLOCK:]], axis=0)
    factor = jnp.exp2(logs - peak)
    total = both[:, HEAD_DIM:] + factor
    mean = (both[:, :HEAD_DIM] + factor * rows(mean_ref)) / total
    return mean, total, peak


def near_kernel(after_1, after_2, after_3, after_4, core_ref, q_ref, up_1_ref, up_2_ref, inner_ref, mine_ref, theirs_ref, mean_ref, log_ref, *refs):
    new_mean_ref, new_log_ref, keys_ref, values_ref = refs
    keys_ref[...] = halve(inner_ref[0])
    values_ref[...] = halve(inner_ref[1])
    by_core(core_ref, functools.partial(near_body, q_ref, inner_ref, mine_ref, theirs_ref, mean_ref, log_ref, new_mean_ref, new_log_ref, up_1_ref, up_2_ref, keys_ref, values_ref))


def near_body(q_ref, inner_ref, mine_ref, theirs_ref, mean_ref, log_ref, new_mean_ref, new_log_ref, up_1_ref, up_2_ref, keys_ref, values_ref, edge, other):
    for head in range(HEADS):
        cols = slice(head * HEAD_DIM, (head + 1) * HEAD_DIM)
        mean, total, peak = attend(
            other,
            edge,
            cols,
            (q_ref, inner_ref[0, edge, cols], inner_ref[1, edge, cols]),
            None,
            [
                (up_1_ref, keys_ref[:, cols], values_ref[:, cols], 1.0),
                (
                    up_2_ref,
                    jnp.concatenate([mine_ref[0, :, cols], theirs_ref[0, :, cols]], 0),
                    jnp.concatenate([mine_ref[1, :, cols], theirs_ref[1, :, cols]], 0),
                    2.0,
                ),
            ],
            mean_ref,
            log_ref,
        )
        logs = jnp.log2(total) + peak
        new_mean_ref[other, cols] = mean[:BLOCK]
        new_mean_ref[edge, cols] = mean[BLOCK:]
        new_log_ref[other, cols] = logs[:BLOCK]
        new_log_ref[edge, cols] = logs[BLOCK:]


def far_kernel(core_ref, q_ref, edge_ref, mine_ref, theirs_ref, mean_ref, log_ref, *refs):
    out_ref = refs[-1]
    count = len(refs) // 2 + 1
    up_refs = refs[:count]
    more_refs = refs[count:-1]
    by_core(core_ref, functools.partial(far_body, core_ref,q_ref, edge_ref, mine_ref, theirs_ref, mean_ref, log_ref, up_refs, more_refs, out_ref))


def far_body(core_ref,q_ref, edge_ref, mine_ref, theirs_ref, mean_ref, log_ref, up_refs, more_refs, out_ref, edge, other):
    bias = jnp.where(core_ref[1] == 1, 0.0, neg_large)
    for head in range(HEADS):
        cols = slice(head * HEAD_DIM, (head + 1) * HEAD_DIM)

        def parts(which, level):
            part = slice(64 * (level - 3), 64 * (level - 2))
            return jnp.concatenate([mine_ref[which, part, cols], theirs_ref[which, part, cols]], 0)

        coarse = [
            (up_refs[level - 3], parts(0, level), parts(1, level), float(level))
            for level in (3, 4)
        ]
        for level, more_ref in enumerate(more_refs, 5):
            coarse.append(
                (up_refs[level - 3], more_ref[0, :, cols], more_ref[1, :, cols], float(level))
            )
        mean, _, _ = attend(
            edge,
            other,
            cols,
            (q_ref, edge_ref[0, :, cols], edge_ref[1, :, cols]),
            bias,
            coarse,
            mean_ref,
            log_ref,
        )
        mean = mean.astype(out_ref.dtype)
        out_ref[edge, cols] = mean[:BLOCK]
        out_ref[other, cols] = mean[BLOCK:]


def call(kernel, in_specs, outputs, name, micros, *inputs, scratch=(), aliases=()):
    return pl.pallas_call(
        kernel,
        in_specs=in_specs,
        out_specs=[VMEM] * len(outputs),
        out_shape=[jax.ShapeDtypeStruct(shape, dtype) for shape, dtype in outputs],
        scratch_shapes=[pltpu.VMEM(shape, dtype) for shape, dtype in scratch],
        cost_estimate=pl.CostEstimate(
            flops=micros * 1_000_000_000, bytes_accessed=0, transcendentals=0
        ),
        input_output_aliases=dict(aliases),
        compiler_params=pltpu.CompilerParams(vmem_limit_bytes=16 << 20),
        name=name,
    )(*inputs)


def sent(array, stride):
    count = lax.axis_size("seq")
    return lax.ppermute(array, "seq", [(i, i ^ stride) for i in range(count)])


def halve_rows(pairs):
    wide = pairs.reshape(2, pairs.shape[1] // 2, 2, pairs.shape[2]).astype(jnp.float32)
    return ((wide[:, :, 0] + wide[:, :, 1]) * 0.5).astype(jnp.bfloat16)


def on_device(queries, keyval):
    count = lax.axis_size("seq")
    levels = count.bit_length() - 1
    index = lax.axis_index("seq")
    core = index % 2
    inside = jnp.where(core == 0, index > 0, index < count - 1)
    position = jnp.stack((core, inside.astype(core.dtype)))
    rows, features = queries.shape
    narrow = keyval.dtype
    wide = ((rows, features), jnp.float32)
    up = ((rows, features), narrow)

    def some(count):
        return ((2, count, features), narrow)

    edge, own_2, own_3, own_4 = call(
        own_pool_kernel,
        [SMEM, VMEM],
        [some(BLOCK), some(64), some(32), some(16)],
        "pool",
        0,
        position,
        keyval,
    )
    side_2 = sent(own_2, 2)
    inner = sent(keyval, 1)
    early = [sent(own_3, 4), sent(own_4, 8), sent(own_4, 12)]
    edge, side_3, side_4 = call(
        side_pool_kernel,
        [ANY] * 3 + [VMEM] * 2,
        [some(BLOCK), some(32), some(16)],
        "side",
        0,
        *early,
        edge,
        side_2,
        aliases={3: 0},
    )
    links = [(i, i + 1) for i in range(1, count - 1, 2)]
    edge = lax.ppermute(edge, "seq", links + [(j, i) for i, j in links])
    late = [sent(side_3, 4), sent(side_4, 8), sent(side_4, 12)]
    other_2 = sent(side_2, 1)
    mean, log = call(
        own_kernel, [ANY] + [VMEM] * 2, [wide, wide], "own", 0, side_3, queries, keyval
    )
    up_1, up_2, *ups = call(ups_kernel, [ANY, VMEM], [up] * levels, "ups", 0, side_3, queries)
    mean, log = call(
        near_kernel,
        [ANY] * 4 + [SMEM] + [VMEM] * 8,
        [wide, wide],
        "near",
        0,
        *early,
        side_3,
        position,
        queries,
        up_1,
        up_2,
        inner,
        side_2,
        other_2,
        mean,
        log,
        scratch=[((BLOCK, features), narrow), ((BLOCK, features), narrow)],
    )
    pieces = (early[0], late[0], early[1], early[2], late[1], late[2])
    (late,) = call(join_kernel, [ANY] * 2 + [VMEM] * 6, [some(128)], "join", 0, edge, log, *pieces)
    their_late = sent(late, 1)
    more = []
    if levels > 4:
        own = halve_rows(halve_rows(jnp.concatenate((keyval, inner), axis=1)))
        own = halve_rows(jnp.concatenate((own, side_2, other_2), axis=1))
        own = jnp.concatenate((own, late[:, :64], their_late[:, :64]), axis=1)
        own = jnp.concatenate((halve_rows(own), late[:, 64:], their_late[:, 64:]), axis=1)
        own = halve_rows(own)
        for level in range(5, levels + 1):
            more.append(sent(own, 1 << level - 1))
            own = halve_rows(jnp.concatenate((own, more[-1]), axis=1))
    far = [position, queries, edge, late, their_late, mean, log] + ups + more
    return call(far_kernel, [SMEM] + [VMEM] * (len(far) - 1), [up], "far", 0, *far)[0]


def solution(mesh):
    return jax.shard_map(
        on_device,
        mesh=mesh,
        in_specs=(P(("streams", "seq"), None), P(None, ("streams", "seq"), None)),
        out_specs=P(("streams", "seq"), None),
        check_vma=False,
    )
```

```python
import functools
import math

import jax
import jax.numpy as jnp
from jax import lax
from jax.experimental import pallas as pl
from jax.experimental.pallas import tpu as pltpu
from jax.sharding import PartitionSpec as P

HEADS = 16
HEAD_DIM = 128
BLOCK = 128
GROUP = 8
neg_large = -1e30
log_two = 0.6931471805599453
to_log2 = 1.0 / (math.sqrt(HEAD_DIM) * log_two)
VMEM = pl.BlockSpec(memory_space=pltpu.VMEM)
ANY = pl.BlockSpec(memory_space=pl.ANY)
SMEM = pl.BlockSpec(memory_space=pltpu.SMEM)


def dot(left, right):
    return lax.dot_general(
        left, right, (((1,), (0,)), ((), ())), preferred_element_type=jnp.float32
    )


def dot_t(left, right):
    return lax.dot_general(
        left, right, (((1,), (1,)), ((), ())), preferred_element_type=jnp.float32
    )


def iota(shape, dim):
    return lax.broadcasted_iota(jnp.int32, shape, dim)


def halve(rows):
    shape = (rows.shape[0] // 2, rows.shape[0])
    pairs = jnp.where(iota(shape, 1) >> 1 == iota(shape, 0), 0.5, 0.0).astype(jnp.bfloat16)
    return dot(pairs, rows).astype(jnp.bfloat16)


def repeated_halve(rows, level):
    count = rows.shape[0]
    shape = (count, count)
    first = iota(shape, 0) >> level << level
    hit = (iota(shape, 1) == first) | (iota(shape, 1) == first + (1 << level - 1))
    return dot(jnp.where(hit, 0.5, 0.0).astype(jnp.bfloat16), rows).astype(jnp.bfloat16)


def with_ones(values):
    return jnp.concatenate([values, jnp.ones(values.shape, values.dtype)], axis=1)


def row_max(scores):
    return jnp.max(scores, axis=1, keepdims=True)


def own_pool_kernel(core_ref, kv_ref, edge_ref, *out_refs):
    outer = pl.ds(pl.multiple_of(core_ref[0] * BLOCK, BLOCK), BLOCK)
    edge_ref[...] = kv_ref[:, outer, :]
    for which in range(2):
        rows = halve(kv_ref[which])
        for out_ref in out_refs:
            rows = halve(rows)
            out_ref[which] = rows


def side_pool_kernel(*refs):
    kv_ref, _, *out_refs = refs[-4:]
    for which in range(2):
        rows = kv_ref[which]
        for out_ref in out_refs:
            rows = halve(rows)
            out_ref[which] = rows


def join_kernel(after_1, after_2, *refs):
    start = 0
    for ref in refs[:-1]:
        refs[-1][:, start : start + ref.shape[1], :] = ref[...]
        start += ref.shape[1]


def ups_kernel(after_ref, q_ref, *refs):
    up = q_ref[...]
    for level, ref in enumerate(refs, 1):
        up = repeated_halve(up, level)
        ref[...] = up


def own_kernel(after_ref, q_ref, kv_ref, mean_ref, log_ref):
    for head in range(HEADS):
        cols = slice(head * HEAD_DIM, (head + 1) * HEAD_DIM)
        scores = dot_t(q_ref[:, cols], kv_ref[0, :, cols])
        peak = row_max(scores) * to_log2
        weights = jnp.exp2(scores * to_log2 - peak).astype(jnp.bfloat16)
        both = dot(weights, with_ones(kv_ref[1, :, cols]))
        total = both[:, HEAD_DIM:]
        mean_ref[:, cols] = both[:, :HEAD_DIM] / total
        log_ref[:, cols] = jnp.log2(total) + peak


def by_core(core_ref, body):
    blocks = slice(0, BLOCK), slice(BLOCK, 2 * BLOCK)

    @pl.when(core_ref[0] == 0)
    def _():
        body(*blocks)

    @pl.when(core_ref[0] == 1)
    def _():
        body(*blocks[::-1])


def attend(first, second, cols, fine, coarse, mean_ref, log_ref):
    def rows(ref):
        return jnp.concatenate([ref[first, cols], ref[second, cols]], axis=0)

    scores = [dot_t(rows(level[0]), level[1]) for level in coarse]
    peak = functools.reduce(jnp.maximum, scores)
    if fine is not None:
        query_ref, key, value = fine
        near = dot_t(query_ref[first, cols], key)
        peak = jnp.concatenate([jnp.maximum(peak[:BLOCK], near), peak[BLOCK:]], axis=0)
    logs = rows(log_ref)
    peak = jnp.maximum(row_max(peak) * to_log2, logs)
    weights = [
        jnp.exp2(score * to_log2 - (peak - level)).astype(jnp.bfloat16)
        for score, (_, _, _, level) in zip(scores, coarse)
    ]
    values = jnp.concatenate([level[2] for level in coarse], axis=0)
    both = dot(jnp.concatenate(weights, axis=1), with_ones(values))
    if fine is not None:
        weights = jnp.exp2(near * to_log2 - peak[:BLOCK]).astype(jnp.bfloat16)
        near = dot(weights, with_ones(value))
        both = jnp.concatenate([both[:BLOCK] + near, both[BLOCK:]], axis=0)
    factor = jnp.exp2(logs - peak)
    total = both[:, HEAD_DIM:] + factor
    mean = (both[:, :HEAD_DIM] + factor * rows(mean_ref)) / total
    return mean, total, peak


def near_kernel(after_1, after_2, after_3, after_4, core_ref, q_ref, up_1_ref, up_2_ref, inner_ref, mine_ref, their_key_ref, their_value_ref, mean_ref, log_ref, *refs):
    new_mean_ref, new_log_ref, keys_ref, values_ref = refs
    keys_ref[...] = halve(inner_ref[0])
    values_ref[...] = halve(inner_ref[1])
    by_core(core_ref, functools.partial(near_body, q_ref, inner_ref, mine_ref, their_key_ref, their_value_ref, mean_ref, log_ref, new_mean_ref, new_log_ref, up_1_ref, up_2_ref, keys_ref, values_ref))


def near_body(q_ref, inner_ref, mine_ref, their_key_ref, their_value_ref, mean_ref, log_ref, new_mean_ref, new_log_ref, up_1_ref, up_2_ref, keys_ref, values_ref, edge, other):
    for head in range(HEADS):
        cols = slice(head * HEAD_DIM, (head + 1) * HEAD_DIM)
        mean, total, peak = attend(
            other,
            edge,
            cols,
            (q_ref, inner_ref[0, edge, cols], inner_ref[1, edge, cols]),
            [
                (up_1_ref, keys_ref[:, cols], values_ref[:, cols], 1.0),
                (
                    up_2_ref,
                    jnp.concatenate([mine_ref[0, :, cols], their_key_ref[0, :, cols]], 0),
                    jnp.concatenate([mine_ref[1, :, cols], their_value_ref[0, :, cols]], 0),
                    2.0,
                ),
            ],
            mean_ref,
            log_ref,
        )
        logs = jnp.log2(total) + peak
        new_mean_ref[other, cols] = mean[:BLOCK]
        new_mean_ref[edge, cols] = mean[BLOCK:]
        new_log_ref[other, cols] = logs[:BLOCK]
        new_log_ref[edge, cols] = logs[BLOCK:]


def edge_kernel(after_ref, core_ref, q_ref, edge_ref, mean_ref, log_ref, new_mean_ref, new_log_ref):
    bias = jnp.where(core_ref[1] == 1, 0.0, neg_large)

    def body(edge, other):
        spans = [slice(head * HEAD_DIM, (head + 1) * HEAD_DIM) for head in range(HEADS)]
        scores = [dot_t(q_ref[edge, cols], edge_ref[0, :, cols]) + bias for cols in spans]
        logs = [log_ref[edge, cols] for cols in spans]
        peaks = [
            jnp.maximum(row_max(score) * to_log2, log) for score, log in zip(scores, logs)
        ]
        weights = [
            jnp.exp2(score * to_log2 - peak).astype(jnp.bfloat16)
            for score, peak in zip(scores, peaks)
        ]
        boths = [
            dot(weight, with_ones(edge_ref[1, :, cols])) for weight, cols in zip(weights, spans)
        ]
        means = []
        for cols, log, peak, both in zip(spans, logs, peaks, boths):
            factor = jnp.exp2(log - peak)
            total = both[:, HEAD_DIM:] + factor
            sums = both[:, :HEAD_DIM] + factor * mean_ref[edge, cols]
            means.append((sums / total, jnp.log2(total) + peak))
        for cols, (mean, log) in zip(spans, means):
            new_mean_ref[edge, cols] = mean
            new_log_ref[edge, cols] = log

    by_core(core_ref, body)


def far_kernel(mine_ref, theirs_ref, mean_ref, log_ref, *refs):
    out_ref = refs[-1]
    count = len(refs) // 2 + 1
    up_refs = refs[:count]
    more_refs = refs[count:-1]

    def parts(which, level, cols):
        if level > 4:
            return more_refs[level - 5][which, :, cols]
        part = slice(64 * (level - 3), 64 * (level - 2))
        return jnp.concatenate([mine_ref[which, part, cols], theirs_ref[which, part, cols]], 0)

    levels = range(3, 3 + count)
    for start in range(0, HEADS, GROUP):
        spans = [
            slice(head * HEAD_DIM, (head + 1) * HEAD_DIM) for head in range(start, start + GROUP)
        ]
        scores = [
            [dot_t(up_refs[level - 3][:, cols], parts(0, level, cols)) for level in levels]
            for cols in spans
        ]
        logs = [log_ref[:, cols] for cols in spans]
        peaks = [
            jnp.maximum(row_max(functools.reduce(jnp.maximum, score)) * to_log2, log)
            for score, log in zip(scores, logs)
        ]
        weights = [
            [
                jnp.exp2(part * to_log2 - (peak - float(level))).astype(jnp.bfloat16)
                for level, part in zip(levels, score)
            ]
            for score, peak in zip(scores, peaks)
        ]
        boths = [
            dot(
                jnp.concatenate(weight, axis=1),
                with_ones(jnp.concatenate([parts(1, level, cols) for level in levels], axis=0)),
            )
            for weight, cols in zip(weights, spans)
        ]
        for cols, log, peak, both in zip(spans, logs, peaks, boths):
            factor = jnp.exp2(log - peak)
            total = both[:, HEAD_DIM:] + factor
            sums = both[:, :HEAD_DIM] + factor * mean_ref[:, cols]
            out_ref[:, cols] = (sums / total).astype(out_ref.dtype)


def call(kernel, in_specs, outputs, name, micros, *inputs, scratch=(), aliases=()):
    return pl.pallas_call(
        kernel,
        in_specs=in_specs,
        out_specs=[VMEM] * len(outputs),
        out_shape=[jax.ShapeDtypeStruct(shape, dtype) for shape, dtype in outputs],
        scratch_shapes=[pltpu.VMEM(shape, dtype) for shape, dtype in scratch],
        cost_estimate=pl.CostEstimate(
            flops=micros * 1_000_000_000, bytes_accessed=0, transcendentals=0
        ),
        input_output_aliases=dict(aliases),
        compiler_params=pltpu.CompilerParams(vmem_limit_bytes=16 << 20),
        name=name,
    )(*inputs)


def sent(array, stride):
    count = lax.axis_size("seq")
    return lax.ppermute(array, "seq", [(i, i ^ stride) for i in range(count)])


def halve_rows(pairs):
    wide = pairs.reshape(2, pairs.shape[1] // 2, 2, pairs.shape[2]).astype(jnp.float32)
    return ((wide[:, :, 0] + wide[:, :, 1]) * 0.5).astype(jnp.bfloat16)


def on_device(queries, keyval):
    count = lax.axis_size("seq")
    levels = count.bit_length() - 1
    index = lax.axis_index("seq")
    core = index % 2
    inside = jnp.where(core == 0, index > 0, index < count - 1)
    position = jnp.stack((core, inside.astype(core.dtype)))
    rows, features = queries.shape
    narrow = keyval.dtype
    wide = ((rows, features), jnp.float32)
    up = ((rows, features), narrow)

    def some(count):
        return ((2, count, features), narrow)

    edge, own_2, own_3, own_4 = call(
        own_pool_kernel,
        [SMEM, VMEM],
        [some(BLOCK), some(64), some(32), some(16)],
        "pool",
        0,
        position,
        keyval,
    )
    side_2 = sent(own_2, 2)
    inner = sent(keyval, 1)
    early = [sent(own_3, 4), sent(own_4, 8), sent(own_4, 12)]
    edge, side_3, side_4 = call(
        side_pool_kernel,
        [ANY] * 3 + [VMEM] * 2,
        [some(BLOCK), some(32), some(16)],
        "side",
        0,
        *early,
        edge,
        side_2,
        aliases={3: 0},
    )
    links = [(i, i + 1) for i in range(1, count - 1, 2)]
    edge = lax.ppermute(edge, "seq", links + [(j, i) for i, j in links])
    late = [sent(side_3, 4), sent(side_4, 8), sent(side_4, 12)]
    other_2 = [sent(side_2[which : which + 1], 1) for which in range(2)]
    mean, log = call(
        own_kernel, [ANY] + [VMEM] * 2, [wide, wide], "own", 0, side_3, queries, keyval
    )
    up_1, up_2, *ups = call(ups_kernel, [ANY, VMEM], [up] * levels, "ups", 0, side_3, queries)
    mean, log = call(
        near_kernel,
        [ANY] * 4 + [SMEM] + [VMEM] * 9,
        [wide, wide],
        "near",
        0,
        *early,
        side_3,
        position,
        queries,
        up_1,
        up_2,
        inner,
        side_2,
        *other_2,
        mean,
        log,
        scratch=[((BLOCK, features), narrow), ((BLOCK, features), narrow)],
    )
    pieces = (early[0], late[0], early[1], early[2], late[1], late[2])
    (late,) = call(join_kernel, [ANY] * 2 + [VMEM] * 6, [some(128)], "join", 0, edge, log, *pieces)
    their_late = sent(late, 1)
    more = []
    if levels > 4:
        own = halve_rows(halve_rows(jnp.concatenate((keyval, inner), axis=1)))
        own = halve_rows(jnp.concatenate((own, side_2, jnp.concatenate(other_2)), axis=1))
        own = jnp.concatenate((own, late[:, :64], their_late[:, :64]), axis=1)
        own = jnp.concatenate((halve_rows(own), late[:, 64:], their_late[:, 64:]), axis=1)
        own = halve_rows(own)
        for level in range(5, levels + 1):
            more.append(sent(own, 1 << level - 1))
            own = halve_rows(jnp.concatenate((own, more[-1]), axis=1))
    mean, log = call(
        edge_kernel,
        [ANY, SMEM] + [VMEM] * 4,
        [wide, wide],
        "edge",
        0,
        late,
        position,
        queries,
        edge,
        mean,
        log,
        aliases={4: 0, 5: 1},
    )
    far = [late, their_late, mean, log] + ups + more
    return call(far_kernel, [VMEM] * len(far), [up], "far", 0, *far)[0]


def solution(mesh):
    return jax.shard_map(
        on_device,
        mesh=mesh,
        in_specs=(P(("streams", "seq"), None), P(None, ("streams", "seq"), None)),
        out_specs=P(("streams", "seq"), None),
        check_vma=False,
    )
```

```python
import functools
import math

import jax
import jax.numpy as jnp
from jax import lax
from jax.experimental import pallas as pl
from jax.experimental.pallas import tpu as pltpu
from jax.sharding import PartitionSpec as P

HEADS = 16
HEAD_DIM = 128
BLOCK = 128
GROUP = 8
neg_large = -1e30
log_two = 0.6931471805599453
to_log2 = 1.0 / (math.sqrt(HEAD_DIM) * log_two)
VMEM = pl.BlockSpec(memory_space=pltpu.VMEM)
ANY = pl.BlockSpec(memory_space=pl.ANY)
SMEM = pl.BlockSpec(memory_space=pltpu.SMEM)


def dot(left, right):
    return lax.dot_general(
        left, right, (((1,), (0,)), ((), ())), preferred_element_type=jnp.float32
    )


def dot_t(left, right):
    return lax.dot_general(
        left, right, (((1,), (1,)), ((), ())), preferred_element_type=jnp.float32
    )


def iota(shape, dim):
    return lax.broadcasted_iota(jnp.int32, shape, dim)


def halve(rows):
    shape = (rows.shape[0] // 2, rows.shape[0])
    pairs = jnp.where(iota(shape, 1) >> 1 == iota(shape, 0), 0.5, 0.0).astype(jnp.bfloat16)
    return dot(pairs, rows).astype(jnp.bfloat16)


def repeated_halve(rows, level):
    count = rows.shape[0]
    shape = (count, count)
    first = iota(shape, 0) >> level << level
    hit = (iota(shape, 1) == first) | (iota(shape, 1) == first + (1 << level - 1))
    return dot(jnp.where(hit, 0.5, 0.0).astype(jnp.bfloat16), rows).astype(jnp.bfloat16)


def with_ones(values):
    return jnp.concatenate([values, jnp.ones(values.shape, values.dtype)], axis=1)


def row_max(scores):
    return jnp.max(scores, axis=1, keepdims=True)


def rim_kernel(after_ref, core_ref, kv_ref, edge_ref):
    outer = pl.ds(pl.multiple_of(core_ref[0] * BLOCK, BLOCK), BLOCK)
    edge_ref[...] = kv_ref[:, outer, :]


def own_pool_kernel(kv_ref, *out_refs):
    for which in range(2):
        rows = halve(kv_ref[which])
        for out_ref in out_refs:
            rows = halve(rows)
            out_ref[which] = rows


def side_pool_kernel(*refs):
    kv_ref, _, *out_refs = refs[-4:]
    for which in range(2):
        rows = kv_ref[which]
        for out_ref in out_refs:
            rows = halve(rows)
            out_ref[which] = rows


def join_kernel(after_1, after_2, *refs):
    start = 0
    for ref in refs[:-1]:
        refs[-1][:, start : start + ref.shape[1], :] = ref[...]
        start += ref.shape[1]


def ups_kernel(after_ref, q_ref, *refs):
    up = q_ref[...]
    for level, ref in enumerate(refs, 1):
        up = repeated_halve(up, level)
        ref[...] = up


def own_kernel(after_ref, q_ref, kv_ref, mean_ref, log_ref):
    for head in range(HEADS):
        cols = slice(head * HEAD_DIM, (head + 1) * HEAD_DIM)
        scores = dot_t(q_ref[:, cols], kv_ref[0, :, cols])
        peak = row_max(scores) * to_log2
        weights = jnp.exp2(scores * to_log2 - peak).astype(jnp.bfloat16)
        both = dot(weights, with_ones(kv_ref[1, :, cols]))
        total = both[:, HEAD_DIM:]
        mean_ref[:, cols] = both[:, :HEAD_DIM] / total
        log_ref[:, cols] = jnp.log2(total) + peak


def by_core(core_ref, body):
    blocks = slice(0, BLOCK), slice(BLOCK, 2 * BLOCK)

    @pl.when(core_ref[0] == 0)
    def _():
        body(*blocks)

    @pl.when(core_ref[0] == 1)
    def _():
        body(*blocks[::-1])


def attend(first, second, cols, fine, coarse, mean_ref, log_ref):
    def rows(ref):
        return jnp.concatenate([ref[first, cols], ref[second, cols]], axis=0)

    scores = [dot_t(rows(level[0]), level[1]) for level in coarse]
    peak = functools.reduce(jnp.maximum, scores)
    if fine is not None:
        query_ref, key, value = fine
        near = dot_t(query_ref[first, cols], key)
        peak = jnp.concatenate([jnp.maximum(peak[:BLOCK], near), peak[BLOCK:]], axis=0)
    logs = rows(log_ref)
    peak = jnp.maximum(row_max(peak) * to_log2, logs)
    weights = [
        jnp.exp2(score * to_log2 - (peak - level)).astype(jnp.bfloat16)
        for score, (_, _, _, level) in zip(scores, coarse)
    ]
    values = jnp.concatenate([level[2] for level in coarse], axis=0)
    both = dot(jnp.concatenate(weights, axis=1), with_ones(values))
    if fine is not None:
        weights = jnp.exp2(near * to_log2 - peak[:BLOCK]).astype(jnp.bfloat16)
        near = dot(weights, with_ones(value))
        both = jnp.concatenate([both[:BLOCK] + near, both[BLOCK:]], axis=0)
    factor = jnp.exp2(logs - peak)
    total = both[:, HEAD_DIM:] + factor
    mean = (both[:, :HEAD_DIM] + factor * rows(mean_ref)) / total
    return mean, total, peak


def near_kernel(after_1, after_2, after_3, after_4, core_ref, q_ref, up_1_ref, up_2_ref, inner_ref, mine_ref, their_key_ref, their_value_ref, mean_ref, log_ref, *refs):
    new_mean_ref, new_log_ref, keys_ref, values_ref = refs
    keys_ref[...] = halve(inner_ref[0])
    values_ref[...] = halve(inner_ref[1])
    by_core(core_ref, functools.partial(near_body, q_ref, inner_ref, mine_ref, their_key_ref, their_value_ref, mean_ref, log_ref, new_mean_ref, new_log_ref, up_1_ref, up_2_ref, keys_ref, values_ref))


def near_body(q_ref, inner_ref, mine_ref, their_key_ref, their_value_ref, mean_ref, log_ref, new_mean_ref, new_log_ref, up_1_ref, up_2_ref, keys_ref, values_ref, edge, other):
    for head in range(HEADS):
        cols = slice(head * HEAD_DIM, (head + 1) * HEAD_DIM)
        mean, total, peak = attend(
            other,
            edge,
            cols,
            (q_ref, inner_ref[0, edge, cols], inner_ref[1, edge, cols]),
            [
                (up_1_ref, keys_ref[:, cols], values_ref[:, cols], 1.0),
                (
                    up_2_ref,
                    jnp.concatenate([mine_ref[0, :, cols], their_key_ref[0, :, cols]], 0),
                    jnp.concatenate([mine_ref[1, :, cols], their_value_ref[0, :, cols]], 0),
                    2.0,
                ),
            ],
            mean_ref,
            log_ref,
        )
        logs = jnp.log2(total) + peak
        new_mean_ref[other, cols] = mean[:BLOCK]
        new_mean_ref[edge, cols] = mean[BLOCK:]
        new_log_ref[other, cols] = logs[:BLOCK]
        new_log_ref[edge, cols] = logs[BLOCK:]


def edge_kernel(after_ref, core_ref, q_ref, edge_ref, mean_ref, log_ref, new_mean_ref, new_log_ref):
    bias = jnp.where(core_ref[1] == 1, 0.0, neg_large)

    def body(edge, other):
        spans = [slice(head * HEAD_DIM, (head + 1) * HEAD_DIM) for head in range(HEADS)]
        scores = [dot_t(q_ref[edge, cols], edge_ref[0, :, cols]) + bias for cols in spans]
        logs = [log_ref[edge, cols] for cols in spans]
        peaks = [
            jnp.maximum(row_max(score) * to_log2, log) for score, log in zip(scores, logs)
        ]
        weights = [
            jnp.exp2(score * to_log2 - peak).astype(jnp.bfloat16)
            for score, peak in zip(scores, peaks)
        ]
        boths = [
            dot(weight, with_ones(edge_ref[1, :, cols])) for weight, cols in zip(weights, spans)
        ]
        means = []
        for cols, log, peak, both in zip(spans, logs, peaks, boths):
            factor = jnp.exp2(log - peak)
            total = both[:, HEAD_DIM:] + factor
            sums = both[:, :HEAD_DIM] + factor * mean_ref[edge, cols]
            means.append((sums / total, jnp.log2(total) + peak))
        for cols, (mean, log) in zip(spans, means):
            new_mean_ref[:, cols] = mean
            new_log_ref[:, cols] = log

    by_core(core_ref, body)


def far_kernel(core_ref, *refs):
    by_core(core_ref, functools.partial(far_body, *refs))


def far_body(
    mine_ref, theirs_ref, mean_ref, log_ref, edge_mean_ref, edge_log_ref, *refs
):
    *refs, hbm_ref, out_ref, sems, edge, other = refs
    count = (len(refs) + 2) // 2
    up_refs = refs[:count]
    more_refs = refs[count:]
    copies = []

    def parts(which, level, cols):
        if level > 4:
            return more_refs[level - 5][which, :, cols]
        part = slice(64 * (level - 3), 64 * (level - 2))
        return jnp.concatenate([mine_ref[which, part, cols], theirs_ref[which, part, cols]], 0)

    def state(ref, edge_ref, cols):
        pair = [edge_ref[:, cols], ref[other, cols]]
        return jnp.concatenate(pair if edge.start == 0 else pair[::-1], axis=0)

    levels = range(3, 3 + count)
    for start in range(0, HEADS, GROUP):
        spans = [
            slice(head * HEAD_DIM, (head + 1) * HEAD_DIM) for head in range(start, start + GROUP)
        ]
        scores = [
            [dot_t(up_refs[level - 3][:, cols], parts(0, level, cols)) for level in levels]
            for cols in spans
        ]
        logs = [state(log_ref, edge_log_ref, cols) for cols in spans]
        peaks = [
            jnp.maximum(row_max(functools.reduce(jnp.maximum, score)) * to_log2, log)
            for score, log in zip(scores, logs)
        ]
        weights = [
            [
                jnp.exp2(part * to_log2 - (peak - float(level))).astype(jnp.bfloat16)
                for level, part in zip(levels, score)
            ]
            for score, peak in zip(scores, peaks)
        ]
        boths = [
            dot(
                jnp.concatenate(weight, axis=1),
                with_ones(jnp.concatenate([parts(1, level, cols) for level in levels], axis=0)),
            )
            for weight, cols in zip(weights, spans)
        ]
        for cols, log, peak, both in zip(spans, logs, peaks, boths):
            factor = jnp.exp2(log - peak)
            total = both[:, HEAD_DIM:] + factor
            sums = both[:, :HEAD_DIM] + factor * state(mean_ref, edge_mean_ref, cols)
            out_ref[:, cols] = (sums / total).astype(out_ref.dtype)
        done = slice(start * HEAD_DIM, (start + GROUP) * HEAD_DIM)
        copies.append(
            pltpu.make_async_copy(
                out_ref.at[:, done], hbm_ref.at[:, done], sems.at[start // GROUP]
            )
        )
        copies[-1].start()
    for copy in copies:
        copy.wait()


def call(kernel, in_specs, outputs, name, micros, *inputs, scratch=(), aliases=(), out_specs=None):
    return pl.pallas_call(
        kernel,
        in_specs=in_specs,
        out_specs=out_specs or [VMEM] * len(outputs),
        out_shape=[jax.ShapeDtypeStruct(shape, dtype) for shape, dtype in outputs],
        scratch_shapes=list(scratch),
        cost_estimate=pl.CostEstimate(
            flops=micros * 1_000_000_000, bytes_accessed=0, transcendentals=0
        ),
        input_output_aliases=dict(aliases),
        compiler_params=pltpu.CompilerParams(vmem_limit_bytes=16 << 20),
        name=name,
    )(*inputs)


def sent(array, stride):
    count = lax.axis_size("seq")
    return lax.ppermute(array, "seq", [(i, i ^ stride) for i in range(count)])


def halve_rows(pairs):
    wide = pairs.reshape(2, pairs.shape[1] // 2, 2, pairs.shape[2]).astype(jnp.float32)
    return ((wide[:, :, 0] + wide[:, :, 1]) * 0.5).astype(jnp.bfloat16)


def on_device(queries, keyval):
    count = lax.axis_size("seq")
    levels = count.bit_length() - 1
    index = lax.axis_index("seq")
    core = index % 2
    inside = jnp.where(core == 0, index > 0, index < count - 1)
    position = jnp.stack((core, inside.astype(core.dtype)))
    rows, features = queries.shape
    narrow = keyval.dtype
    wide = ((rows, features), jnp.float32)
    up = ((rows, features), narrow)

    def some(count):
        return ((2, count, features), narrow)

    own_2, own_3, own_4 = call(
        own_pool_kernel, [VMEM], [some(64), some(32), some(16)], "pool", 0, keyval
    )
    side_2 = sent(own_2, 2)
    inner = sent(keyval, 1)
    early = [sent(own_3, 4), sent(own_4, 8), sent(own_4, 12)]
    (edge,) = call(
        rim_kernel, [ANY, SMEM, VMEM], [some(BLOCK)], "rim", 0, early[1], position, keyval
    )
    edge, side_3, side_4 = call(
        side_pool_kernel,
        [ANY] * 4 + [VMEM],
        [some(BLOCK), some(32), some(16)],
        "side",
        0,
        *early,
        edge,
        side_2,
        aliases={3: 0},
        out_specs=[ANY, VMEM, VMEM],
    )
    links = [(i, i + 1) for i in range(1, count - 1, 2)]
    edge = lax.ppermute(edge, "seq", links + [(j, i) for i, j in links])
    late = [sent(side_3, 4), sent(side_4, 8), sent(side_4, 12)]
    other_2 = [sent(side_2[which : which + 1], 1) for which in range(2)]
    mean, log = call(
        own_kernel, [ANY] + [VMEM] * 2, [wide, wide], "own", 0, side_3, queries, keyval
    )
    up_1, up_2, *ups = call(ups_kernel, [ANY, VMEM], [up] * levels, "ups", 0, side_3, queries)
    mean, log = call(
        near_kernel,
        [ANY] * 4 + [SMEM] + [VMEM] * 9,
        [wide, wide],
        "near",
        0,
        *early,
        side_3,
        position,
        queries,
        up_1,
        up_2,
        inner,
        side_2,
        *other_2,
        mean,
        log,
        scratch=[pltpu.VMEM((BLOCK, features), narrow)] * 2,
    )
    pieces = (early[0], late[0], early[1], early[2], late[1], late[2])
    (late,) = call(join_kernel, [ANY] * 2 + [VMEM] * 6, [some(128)], "join", 0, edge, log, *pieces)
    their_late = sent(late, 1)
    more = []
    if levels > 4:
        own = halve_rows(halve_rows(jnp.concatenate((keyval, inner), axis=1)))
        own = halve_rows(jnp.concatenate((own, side_2, jnp.concatenate(other_2)), axis=1))
        own = jnp.concatenate((own, late[:, :64], their_late[:, :64]), axis=1)
        own = jnp.concatenate((halve_rows(own), late[:, 64:], their_late[:, 64:]), axis=1)
        own = halve_rows(own)
        for level in range(5, levels + 1):
            more.append(sent(own, 1 << level - 1))
            own = halve_rows(jnp.concatenate((own, more[-1]), axis=1))
    edge_mean, edge_log = call(
        edge_kernel,
        [ANY, SMEM] + [VMEM] * 4,
        [((BLOCK, features), jnp.float32)] * 2,
        "edge",
        0,
        late,
        position,
        queries,
        edge,
        mean,
        log,
    )
    far = [position, late, their_late, mean, log, edge_mean, edge_log] + ups + more
    return call(
        far_kernel,
        [SMEM] + [VMEM] * (len(far) - 1),
        [up],
        "far",
        0,
        *far,
        scratch=[pltpu.VMEM(*up), pltpu.SemaphoreType.DMA((HEADS // GROUP,))],
        out_specs=[ANY],
    )[0]


def solution(mesh):
    return jax.shard_map(
        on_device,
        mesh=mesh,
        in_specs=(P(("streams", "seq"), None), P(None, ("streams", "seq"), None)),
        out_specs=P(("streams", "seq"), None),
        check_vma=False,
    )
```

```python
import functools
import math

import jax
import jax.numpy as jnp
from jax import lax
from jax.experimental import pallas as pl
from jax.experimental.pallas import tpu as pltpu
from jax.sharding import PartitionSpec as P

HEADS = 16
HEAD_DIM = 128
BLOCK = 128
GROUP = 8
neg_large = -1e30
log_two = 0.6931471805599453
to_log2 = 1.0 / (math.sqrt(HEAD_DIM) * log_two)
VMEM = pl.BlockSpec(memory_space=pltpu.VMEM)
ANY = pl.BlockSpec(memory_space=pl.ANY)
SMEM = pl.BlockSpec(memory_space=pltpu.SMEM)


def dot(left, right):
    return lax.dot_general(
        left, right, (((1,), (0,)), ((), ())), preferred_element_type=jnp.float32
    )


def dot_t(left, right):
    return lax.dot_general(
        left, right, (((1,), (1,)), ((), ())), preferred_element_type=jnp.float32
    )


def iota(shape, dim):
    return lax.broadcasted_iota(jnp.int32, shape, dim)


def halve(rows):
    shape = (rows.shape[0] // 2, rows.shape[0])
    pairs = jnp.where(iota(shape, 1) >> 1 == iota(shape, 0), 0.5, 0.0).astype(jnp.bfloat16)
    return dot(pairs, rows).astype(jnp.bfloat16)


def repeated_halve(rows, level):
    count = rows.shape[0]
    shape = (count, count)
    first = iota(shape, 0) >> level << level
    hit = (iota(shape, 1) == first) | (iota(shape, 1) == first + (1 << level - 1))
    return dot(jnp.where(hit, 0.5, 0.0).astype(jnp.bfloat16), rows).astype(jnp.bfloat16)


def with_ones(values):
    return jnp.concatenate([values, jnp.ones(values.shape, values.dtype)], axis=1)


def row_max(scores):
    return jnp.max(scores, axis=1, keepdims=True)


def rim_kernel(after_ref, core_ref, kv_ref, edge_ref):
    outer = pl.ds(pl.multiple_of(core_ref[0] * BLOCK, BLOCK), BLOCK)
    edge_ref[...] = kv_ref[:, outer, :]


def own_pool_kernel(kv_ref, *out_refs):
    for which in range(2):
        rows = halve(kv_ref[which])
        for out_ref in out_refs:
            rows = halve(rows)
            out_ref[which] = rows


def side_pool_kernel(*refs):
    kv_ref, _, *out_refs = refs[-4:]
    for which in range(2):
        rows = kv_ref[which]
        for out_ref in out_refs:
            rows = halve(rows)
            out_ref[which] = rows


def join_kernel(after_1, after_2, *refs):
    start = 0
    for ref in refs[:-1]:
        refs[-1][:, start : start + ref.shape[1], :] = ref[...]
        start += ref.shape[1]


def ups_kernel(after_ref, q_ref, *refs):
    up = q_ref[...]
    for level, ref in enumerate(refs, 1):
        up = repeated_halve(up, level)
        ref[...] = up


def own_kernel(after_ref, q_ref, kv_ref, mean_ref, log_ref):
    for head in range(HEADS):
        cols = slice(head * HEAD_DIM, (head + 1) * HEAD_DIM)
        scores = dot_t(q_ref[:, cols], kv_ref[0, :, cols])
        peak = row_max(scores) * to_log2
        weights = jnp.exp2(scores * to_log2 - peak).astype(jnp.bfloat16)
        both = dot(weights, with_ones(kv_ref[1, :, cols]))
        total = both[:, HEAD_DIM:]
        mean_ref[:, cols] = both[:, :HEAD_DIM] / total
        log_ref[:, cols] = jnp.log2(total) + peak


def by_core(core_ref, body):
    blocks = slice(0, BLOCK), slice(BLOCK, 2 * BLOCK)

    @pl.when(core_ref[0] == 0)
    def _():
        body(*blocks)

    @pl.when(core_ref[0] == 1)
    def _():
        body(*blocks[::-1])


def attend(first, second, cols, fine, coarse, mean_ref, log_ref):
    def rows(ref):
        return jnp.concatenate([ref[first, cols], ref[second, cols]], axis=0)

    scores = [dot_t(rows(level[0]), level[1]) for level in coarse]
    peak = functools.reduce(jnp.maximum, scores)
    if fine is not None:
        query_ref, key, value = fine
        near = dot_t(query_ref[first, cols], key)
        peak = jnp.concatenate([jnp.maximum(peak[:BLOCK], near), peak[BLOCK:]], axis=0)
    logs = rows(log_ref)
    peak = jnp.maximum(row_max(peak) * to_log2, logs)
    weights = [
        jnp.exp2(score * to_log2 - (peak - level)).astype(jnp.bfloat16)
        for score, (_, _, _, level) in zip(scores, coarse)
    ]
    values = jnp.concatenate([level[2] for level in coarse], axis=0)
    both = dot(jnp.concatenate(weights, axis=1), with_ones(values))
    if fine is not None:
        weights = jnp.exp2(near * to_log2 - peak[:BLOCK]).astype(jnp.bfloat16)
        near = dot(weights, with_ones(value))
        both = jnp.concatenate([both[:BLOCK] + near, both[BLOCK:]], axis=0)
    factor = jnp.exp2(logs - peak)
    total = both[:, HEAD_DIM:] + factor
    mean = (both[:, :HEAD_DIM] + factor * rows(mean_ref)) / total
    return mean, total, peak


def near_kernel(after_1, after_2, after_3, after_4, core_ref, q_ref, up_1_ref, up_2_ref, inner_ref, mine_ref, their_key_ref, their_value_ref, mean_ref, log_ref, *refs):
    new_mean_ref, new_log_ref, keys_ref, values_ref = refs
    keys_ref[...] = halve(inner_ref[0])
    values_ref[...] = halve(inner_ref[1])
    by_core(core_ref, functools.partial(near_body, q_ref, inner_ref, mine_ref, their_key_ref, their_value_ref, mean_ref, log_ref, new_mean_ref, new_log_ref, up_1_ref, up_2_ref, keys_ref, values_ref))


def near_body(q_ref, inner_ref, mine_ref, their_key_ref, their_value_ref, mean_ref, log_ref, new_mean_ref, new_log_ref, up_1_ref, up_2_ref, keys_ref, values_ref, edge, other):
    for head in range(HEADS):
        cols = slice(head * HEAD_DIM, (head + 1) * HEAD_DIM)
        mean, total, peak = attend(
            other,
            edge,
            cols,
            (q_ref, inner_ref[0, edge, cols], inner_ref[1, edge, cols]),
            [
                (up_1_ref, keys_ref[:, cols], values_ref[:, cols], 1.0),
                (
                    up_2_ref,
                    jnp.concatenate([mine_ref[0, :, cols], their_key_ref[0, :, cols]], 0),
                    jnp.concatenate([mine_ref[1, :, cols], their_value_ref[0, :, cols]], 0),
                    2.0,
                ),
            ],
            mean_ref,
            log_ref,
        )
        logs = jnp.log2(total) + peak
        new_mean_ref[other, cols] = mean[:BLOCK]
        new_mean_ref[edge, cols] = mean[BLOCK:]
        new_log_ref[other, cols] = logs[:BLOCK]
        new_log_ref[edge, cols] = logs[BLOCK:]


def edge_kernel(after_ref, core_ref, q_ref, edge_ref, mean_ref, log_ref, new_mean_ref, new_log_ref):
    bias = jnp.where(core_ref[1] == 1, 0.0, neg_large)

    def body(edge, other):
        spans = [slice(head * HEAD_DIM, (head + 1) * HEAD_DIM) for head in range(HEADS)]
        scores = [dot_t(q_ref[edge, cols], edge_ref[0, :, cols]) + bias for cols in spans]
        logs = [log_ref[edge, cols] for cols in spans]
        peaks = [
            jnp.maximum(row_max(score) * to_log2, log) for score, log in zip(scores, logs)
        ]
        weights = [
            jnp.exp2(score * to_log2 - peak).astype(jnp.bfloat16)
            for score, peak in zip(scores, peaks)
        ]
        boths = [
            dot(weight, with_ones(edge_ref[1, :, cols])) for weight, cols in zip(weights, spans)
        ]
        means = []
        for cols, log, peak, both in zip(spans, logs, peaks, boths):
            factor = jnp.exp2(log - peak)
            total = both[:, HEAD_DIM:] + factor
            sums = both[:, :HEAD_DIM] + factor * mean_ref[edge, cols]
            means.append((sums / total, jnp.log2(total) + peak))
        for cols, (mean, log) in zip(spans, means):
            new_mean_ref[edge, cols] = mean
            new_log_ref[edge, cols] = log
        new_mean_ref[other, :] = mean_ref[other, :]
        new_log_ref[other, :] = log_ref[other, :]

    by_core(core_ref, body)


def far_kernel(mine_ref, theirs_ref, mean_ref, log_ref, *refs):
    *refs, hbm_ref, out_ref, sems = refs
    count = (len(refs) + 2) // 2
    up_refs = refs[:count]
    more_refs = refs[count:]
    copies = []

    def parts(which, level, cols):
        if level > 4:
            return more_refs[level - 5][which, :, cols]
        part = slice(64 * (level - 3), 64 * (level - 2))
        return jnp.concatenate([mine_ref[which, part, cols], theirs_ref[which, part, cols]], 0)

    levels = range(3, 3 + count)
    for start in range(0, HEADS, GROUP):
        spans = [
            slice(head * HEAD_DIM, (head + 1) * HEAD_DIM) for head in range(start, start + GROUP)
        ]
        scores = [
            [dot_t(up_refs[level - 3][:, cols], parts(0, level, cols)) for level in levels]
            for cols in spans
        ]
        logs = [log_ref[:, cols] for cols in spans]
        peaks = [
            jnp.maximum(row_max(functools.reduce(jnp.maximum, score)) * to_log2, log)
            for score, log in zip(scores, logs)
        ]
        weights = [
            [
                jnp.exp2(part * to_log2 - (peak - float(level))).astype(jnp.bfloat16)
                for level, part in zip(levels, score)
            ]
            for score, peak in zip(scores, peaks)
        ]
        boths = [
            dot(
                jnp.concatenate(weight, axis=1),
                with_ones(jnp.concatenate([parts(1, level, cols) for level in levels], axis=0)),
            )
            for weight, cols in zip(weights, spans)
        ]
        for cols, log, peak, both in zip(spans, logs, peaks, boths):
            factor = jnp.exp2(log - peak)
            total = both[:, HEAD_DIM:] + factor
            sums = both[:, :HEAD_DIM] + factor * mean_ref[:, cols]
            out_ref[:, cols] = (sums / total).astype(out_ref.dtype)
        done = slice(start * HEAD_DIM, (start + GROUP) * HEAD_DIM)
        copies.append(
            pltpu.make_async_copy(
                out_ref.at[:, done], hbm_ref.at[:, done], sems.at[start // GROUP]
            )
        )
        copies[-1].start()
    for copy in copies:
        copy.wait()


def call(kernel, in_specs, outputs, name, micros, *inputs, scratch=(), aliases=(), out_specs=None):
    return pl.pallas_call(
        kernel,
        in_specs=in_specs,
        out_specs=out_specs or [VMEM] * len(outputs),
        out_shape=[jax.ShapeDtypeStruct(shape, dtype) for shape, dtype in outputs],
        scratch_shapes=list(scratch),
        cost_estimate=pl.CostEstimate(
            flops=micros * 1_000_000_000, bytes_accessed=0, transcendentals=0
        ),
        input_output_aliases=dict(aliases),
        compiler_params=pltpu.CompilerParams(vmem_limit_bytes=16 << 20),
        name=name,
    )(*inputs)


def sent(array, stride):
    count = lax.axis_size("seq")
    return lax.ppermute(array, "seq", [(i, i ^ stride) for i in range(count)])


def halve_rows(pairs):
    wide = pairs.reshape(2, pairs.shape[1] // 2, 2, pairs.shape[2]).astype(jnp.float32)
    return ((wide[:, :, 0] + wide[:, :, 1]) * 0.5).astype(jnp.bfloat16)


def on_device(queries, keyval):
    count = lax.axis_size("seq")
    levels = count.bit_length() - 1
    index = lax.axis_index("seq")
    core = index % 2
    inside = jnp.where(core == 0, index > 0, index < count - 1)
    position = jnp.stack((core, inside.astype(core.dtype)))
    rows, features = queries.shape
    narrow = keyval.dtype
    wide = ((rows, features), jnp.float32)
    up = ((rows, features), narrow)

    def some(count):
        return ((2, count, features), narrow)

    own_2, own_3, own_4 = call(
        own_pool_kernel, [VMEM], [some(64), some(32), some(16)], "pool", 0, keyval
    )
    side_2 = sent(own_2, 2)
    inner = sent(keyval, 1)
    early = [sent(own_3, 4), sent(own_4, 8), sent(own_4, 12)]
    (edge,) = call(
        rim_kernel, [ANY, SMEM, VMEM], [some(BLOCK)], "rim", 0, early[1], position, keyval
    )
    edge, side_3, side_4 = call(
        side_pool_kernel,
        [ANY] * 4 + [VMEM],
        [some(BLOCK), some(32), some(16)],
        "side",
        0,
        *early,
        edge,
        side_2,
        aliases={3: 0},
        out_specs=[ANY, VMEM, VMEM],
    )
    links = [(i, i + 1) for i in range(1, count - 1, 2)]
    edge = lax.ppermute(edge, "seq", links + [(j, i) for i, j in links])
    late = [sent(side_3, 4), sent(side_4, 8), sent(side_4, 12)]
    other_2 = [sent(side_2[which : which + 1], 1) for which in range(2)]
    mean, log = call(
        own_kernel, [ANY] + [VMEM] * 2, [wide, wide], "own", 0, side_3, queries, keyval
    )
    up_1, up_2, *ups = call(ups_kernel, [ANY, VMEM], [up] * levels, "ups", 0, side_3, queries)
    mean, log = call(
        near_kernel,
        [ANY] * 4 + [SMEM] + [VMEM] * 9,
        [wide, wide],
        "near",
        0,
        *early,
        side_3,
        position,
        queries,
        up_1,
        up_2,
        inner,
        side_2,
        *other_2,
        mean,
        log,
        scratch=[pltpu.VMEM((BLOCK, features), narrow)] * 2,
    )
    pieces = (early[0], late[0], early[1], early[2], late[1], late[2])
    (late,) = call(join_kernel, [ANY] * 2 + [VMEM] * 6, [some(128)], "join", 0, edge, log, *pieces)
    their_late = sent(late, 1)
    more = []
    if levels > 4:
        own = halve_rows(halve_rows(jnp.concatenate((keyval, inner), axis=1)))
        own = halve_rows(jnp.concatenate((own, side_2, jnp.concatenate(other_2)), axis=1))
        own = jnp.concatenate((own, late[:, :64], their_late[:, :64]), axis=1)
        own = jnp.concatenate((halve_rows(own), late[:, 64:], their_late[:, 64:]), axis=1)
        own = halve_rows(own)
        for level in range(5, levels + 1):
            more.append(sent(own, 1 << level - 1))
            own = halve_rows(jnp.concatenate((own, more[-1]), axis=1))
    mean, log = call(
        edge_kernel,
        [ANY, SMEM] + [VMEM] * 4,
        [wide, wide],
        "edge",
        0,
        late,
        position,
        queries,
        edge,
        mean,
        log,
    )
    far = [late, their_late, mean, log] + ups + more
    return call(
        far_kernel,
        [VMEM] * len(far),
        [up],
        "far",
        0,
        *far,
        scratch=[pltpu.VMEM(*up), pltpu.SemaphoreType.DMA((HEADS // GROUP,))],
        out_specs=[ANY],
    )[0]


def solution(mesh):
    return jax.shard_map(
        on_device,
        mesh=mesh,
        in_specs=(P(("streams", "seq"), None), P(None, ("streams", "seq"), None)),
        out_specs=P(("streams", "seq"), None),
        check_vma=False,
    )
```

```python
import functools
import math

import jax
import jax.numpy as jnp
from jax import lax
from jax.experimental import pallas as pl
from jax.experimental.pallas import tpu as pltpu
from jax.sharding import PartitionSpec as P

HEADS = 16
HEAD_DIM = 128
BLOCK = 128
GROUP = 16
neg_large = -1e30
log_two = 0.6931471805599453
to_log2 = 1.0 / (math.sqrt(HEAD_DIM) * log_two)
VMEM = pl.BlockSpec(memory_space=pltpu.VMEM)
ANY = pl.BlockSpec(memory_space=pl.ANY)
SMEM = pl.BlockSpec(memory_space=pltpu.SMEM)


def dot(left, right):
    return lax.dot_general(
        left, right, (((1,), (0,)), ((), ())), preferred_element_type=jnp.float32
    )


def dot_t(left, right):
    return lax.dot_general(
        left, right, (((1,), (1,)), ((), ())), preferred_element_type=jnp.float32
    )


def iota(shape, dim):
    return lax.broadcasted_iota(jnp.int32, shape, dim)


def halve(rows):
    shape = (rows.shape[0] // 2, rows.shape[0])
    pairs = jnp.where(iota(shape, 1) >> 1 == iota(shape, 0), 0.5, 0.0).astype(jnp.bfloat16)
    return dot(pairs, rows).astype(jnp.bfloat16)


def repeated_halve(rows, level):
    count = rows.shape[0]
    shape = (count, count)
    first = iota(shape, 0) >> level << level
    hit = (iota(shape, 1) == first) | (iota(shape, 1) == first + (1 << level - 1))
    return dot(jnp.where(hit, 0.5, 0.0).astype(jnp.bfloat16), rows).astype(jnp.bfloat16)


def with_ones(values):
    return jnp.concatenate([values, jnp.ones(values.shape, values.dtype)], axis=1)


def row_max(scores):
    return jnp.max(scores, axis=1, keepdims=True)


def rim_kernel(after_ref, core_ref, kv_ref, edge_ref):
    outer = pl.ds(pl.multiple_of(core_ref[0] * BLOCK, BLOCK), BLOCK)
    edge_ref[...] = kv_ref[:, outer, :]


def own_pool_kernel(kv_ref, *out_refs):
    for which in range(2):
        rows = halve(kv_ref[which])
        for out_ref in out_refs:
            rows = halve(rows)
            out_ref[which] = rows


def side_pool_kernel(*refs):
    kv_ref, _, *out_refs = refs[-4:]
    for which in range(2):
        rows = kv_ref[which]
        for out_ref in out_refs:
            rows = halve(rows)
            out_ref[which] = rows


def join_kernel(after_1, after_2, *refs):
    start = 0
    for ref in refs[:-1]:
        refs[-1][:, start : start + ref.shape[1], :] = ref[...]
        start += ref.shape[1]


def ups_kernel(after_ref, q_ref, *refs):
    up = q_ref[...]
    for level, ref in enumerate(refs, 1):
        up = repeated_halve(up, level)
        ref[...] = up


def own_kernel(after_ref, q_ref, kv_ref, mean_ref, log_ref):
    for head in range(HEADS):
        cols = slice(head * HEAD_DIM, (head + 1) * HEAD_DIM)
        scores = dot_t(q_ref[:, cols], kv_ref[0, :, cols])
        peak = row_max(scores) * to_log2
        weights = jnp.exp2(scores * to_log2 - peak).astype(jnp.bfloat16)
        both = dot(weights, with_ones(kv_ref[1, :, cols]))
        total = both[:, HEAD_DIM:]
        mean_ref[:, cols] = both[:, :HEAD_DIM] / total
        log_ref[:, cols] = jnp.log2(total) + peak


def by_core(core_ref, body):
    blocks = slice(0, BLOCK), slice(BLOCK, 2 * BLOCK)

    @pl.when(core_ref[0] == 0)
    def _():
        body(*blocks)

    @pl.when(core_ref[0] == 1)
    def _():
        body(*blocks[::-1])


def attend(first, second, cols, fine, coarse, mean_ref, log_ref):
    def rows(ref):
        return jnp.concatenate([ref[first, cols], ref[second, cols]], axis=0)

    scores = [dot_t(rows(level[0]), level[1]) for level in coarse]
    peak = functools.reduce(jnp.maximum, scores)
    if fine is not None:
        query_ref, key, value = fine
        near = dot_t(query_ref[first, cols], key)
        peak = jnp.concatenate([jnp.maximum(peak[:BLOCK], near), peak[BLOCK:]], axis=0)
    logs = rows(log_ref)
    peak = jnp.maximum(row_max(peak) * to_log2, logs)
    weights = [
        jnp.exp2(score * to_log2 - (peak - level)).astype(jnp.bfloat16)
        for score, (_, _, _, level) in zip(scores, coarse)
    ]
    values = jnp.concatenate([level[2] for level in coarse], axis=0)
    both = dot(jnp.concatenate(weights, axis=1), with_ones(values))
    if fine is not None:
        weights = jnp.exp2(near * to_log2 - peak[:BLOCK]).astype(jnp.bfloat16)
        near = dot(weights, with_ones(value))
        both = jnp.concatenate([both[:BLOCK] + near, both[BLOCK:]], axis=0)
    factor = jnp.exp2(logs - peak)
    total = both[:, HEAD_DIM:] + factor
    mean = (both[:, :HEAD_DIM] + factor * rows(mean_ref)) / total
    return mean, total, peak


def near_kernel(after_1, after_2, after_3, after_4, core_ref, q_ref, up_1_ref, up_2_ref, inner_ref, mine_ref, their_key_ref, their_value_ref, mean_ref, log_ref, *refs):
    new_mean_ref, new_log_ref, keys_ref, values_ref = refs
    keys_ref[...] = halve(inner_ref[0])
    values_ref[...] = halve(inner_ref[1])
    by_core(core_ref, functools.partial(near_body, q_ref, inner_ref, mine_ref, their_key_ref, their_value_ref, mean_ref, log_ref, new_mean_ref, new_log_ref, up_1_ref, up_2_ref, keys_ref, values_ref))


def near_body(q_ref, inner_ref, mine_ref, their_key_ref, their_value_ref, mean_ref, log_ref, new_mean_ref, new_log_ref, up_1_ref, up_2_ref, keys_ref, values_ref, edge, other):
    for head in range(HEADS):
        cols = slice(head * HEAD_DIM, (head + 1) * HEAD_DIM)
        mean, total, peak = attend(
            other,
            edge,
            cols,
            (q_ref, inner_ref[0, edge, cols], inner_ref[1, edge, cols]),
            [
                (up_1_ref, keys_ref[:, cols], values_ref[:, cols], 1.0),
                (
                    up_2_ref,
                    jnp.concatenate([mine_ref[0, :, cols], their_key_ref[0, :, cols]], 0),
                    jnp.concatenate([mine_ref[1, :, cols], their_value_ref[0, :, cols]], 0),
                    2.0,
                ),
            ],
            mean_ref,
            log_ref,
        )
        logs = jnp.log2(total) + peak
        new_mean_ref[other, cols] = mean[:BLOCK]
        new_mean_ref[edge, cols] = mean[BLOCK:]
        new_log_ref[other, cols] = logs[:BLOCK]
        new_log_ref[edge, cols] = logs[BLOCK:]


def edge_kernel(after_ref, core_ref, q_ref, edge_ref, mean_ref, log_ref, new_mean_ref, new_log_ref):
    bias = jnp.where(core_ref[1] == 1, 0.0, neg_large)

    def body(edge, other):
        spans = [slice(head * HEAD_DIM, (head + 1) * HEAD_DIM) for head in range(HEADS)]
        scores = [dot_t(q_ref[edge, cols], edge_ref[0, :, cols]) + bias for cols in spans]
        logs = [log_ref[edge, cols] for cols in spans]
        peaks = [
            jnp.maximum(row_max(score) * to_log2, log) for score, log in zip(scores, logs)
        ]
        weights = [
            jnp.exp2(score * to_log2 - peak).astype(jnp.bfloat16)
            for score, peak in zip(scores, peaks)
        ]
        boths = [
            dot(weight, with_ones(edge_ref[1, :, cols])) for weight, cols in zip(weights, spans)
        ]
        means = []
        for cols, log, peak, both in zip(spans, logs, peaks, boths):
            factor = jnp.exp2(log - peak)
            total = both[:, HEAD_DIM:] + factor
            sums = both[:, :HEAD_DIM] + factor * mean_ref[edge, cols]
            means.append((sums / total, jnp.log2(total) + peak))
        for cols, (mean, log) in zip(spans, means):
            new_mean_ref[edge, cols] = mean
            new_log_ref[edge, cols] = log
        new_mean_ref[other, :] = mean_ref[other, :]
        new_log_ref[other, :] = log_ref[other, :]

    by_core(core_ref, body)


def far_kernel(mine_ref, theirs_ref, mean_ref, log_ref, *refs):
    *refs, hbm_ref, out_ref, sems = refs
    count = (len(refs) + 2) // 2
    up_refs = refs[:count]
    more_refs = refs[count:]
    copies = []

    def parts(which, level, cols):
        if level > 4:
            return more_refs[level - 5][which, :, cols]
        part = slice(64 * (level - 3), 64 * (level - 2))
        return jnp.concatenate([mine_ref[which, part, cols], theirs_ref[which, part, cols]], 0)

    levels = range(3, 3 + count)
    for start in range(0, HEADS, GROUP):
        spans = [
            slice(head * HEAD_DIM, (head + 1) * HEAD_DIM) for head in range(start, start + GROUP)
        ]
        scores = [
            [dot_t(up_refs[level - 3][:, cols], parts(0, level, cols)) for level in levels]
            for cols in spans
        ]
        logs = [log_ref[:, cols] for cols in spans]
        peaks = [
            jnp.maximum(row_max(functools.reduce(jnp.maximum, score)) * to_log2, log)
            for score, log in zip(scores, logs)
        ]
        weights = [
            [
                jnp.exp2(part * to_log2 - (peak - float(level))).astype(jnp.bfloat16)
                for level, part in zip(levels, score)
            ]
            for score, peak in zip(scores, peaks)
        ]
        boths = [
            dot(
                jnp.concatenate(weight, axis=1),
                with_ones(jnp.concatenate([parts(1, level, cols) for level in levels], axis=0)),
            )
            for weight, cols in zip(weights, spans)
        ]
        for cols, log, peak, both in zip(spans, logs, peaks, boths):
            factor = jnp.exp2(log - peak)
            total = both[:, HEAD_DIM:] + factor
            sums = both[:, :HEAD_DIM] + factor * mean_ref[:, cols]
            out_ref[:, cols] = (sums / total).astype(out_ref.dtype)
        done = slice(start * HEAD_DIM, (start + GROUP) * HEAD_DIM)
        copies.append(
            pltpu.make_async_copy(
                out_ref.at[:, done], hbm_ref.at[:, done], sems.at[start // GROUP]
            )
        )
        copies[-1].start()
    for copy in copies:
        copy.wait()


def call(kernel, in_specs, outputs, name, micros, *inputs, scratch=(), aliases=(), out_specs=None):
    return pl.pallas_call(
        kernel,
        in_specs=in_specs,
        out_specs=out_specs or [VMEM] * len(outputs),
        out_shape=[jax.ShapeDtypeStruct(shape, dtype) for shape, dtype in outputs],
        scratch_shapes=list(scratch),
        cost_estimate=pl.CostEstimate(
            flops=micros * 1_000_000_000, bytes_accessed=0, transcendentals=0
        ),
        input_output_aliases=dict(aliases),
        compiler_params=pltpu.CompilerParams(vmem_limit_bytes=16 << 20),
        name=name,
    )(*inputs)


def sent(array, stride):
    count = lax.axis_size("seq")
    return lax.ppermute(array, "seq", [(i, i ^ stride) for i in range(count)])


def halve_rows(pairs):
    wide = pairs.reshape(2, pairs.shape[1] // 2, 2, pairs.shape[2]).astype(jnp.float32)
    return ((wide[:, :, 0] + wide[:, :, 1]) * 0.5).astype(jnp.bfloat16)


def on_device(queries, keyval):
    count = lax.axis_size("seq")
    levels = count.bit_length() - 1
    index = lax.axis_index("seq")
    core = index % 2
    inside = jnp.where(core == 0, index > 0, index < count - 1)
    position = jnp.stack((core, inside.astype(core.dtype)))
    rows, features = queries.shape
    narrow = keyval.dtype
    wide = ((rows, features), jnp.float32)
    up = ((rows, features), narrow)

    def some(count):
        return ((2, count, features), narrow)

    own_2, own_3, own_4 = call(
        own_pool_kernel, [VMEM], [some(64), some(32), some(16)], "pool", 0, keyval
    )
    side_2 = sent(own_2, 2)
    inner = sent(keyval, 1)
    early = [sent(own_3, 4), sent(own_4, 8), sent(own_4, 12)]
    (edge,) = call(
        rim_kernel, [ANY, SMEM, VMEM], [some(BLOCK)], "rim", 0, early[1], position, keyval
    )
    edge, side_3, side_4 = call(
        side_pool_kernel,
        [ANY] * 4 + [VMEM],
        [some(BLOCK), some(32), some(16)],
        "side",
        0,
        *early,
        edge,
        side_2,
        aliases={3: 0},
        out_specs=[ANY, VMEM, VMEM],
    )
    links = [(i, i + 1) for i in range(1, count - 1, 2)]
    edge = lax.ppermute(edge, "seq", links + [(j, i) for i, j in links])
    late = [sent(side_3, 4), sent(side_4, 8), sent(side_4, 12)]
    other_2 = [sent(side_2[which : which + 1], 1) for which in range(2)]
    mean, log = call(
        own_kernel, [ANY] + [VMEM] * 2, [wide, wide], "own", 0, side_3, queries, keyval
    )
    up_1, up_2, *ups = call(ups_kernel, [ANY, VMEM], [up] * levels, "ups", 0, side_3, queries)
    mean, log = call(
        near_kernel,
        [ANY] * 4 + [SMEM] + [VMEM] * 9,
        [wide, wide],
        "near",
        0,
        *early,
        side_3,
        position,
        queries,
        up_1,
        up_2,
        inner,
        side_2,
        *other_2,
        mean,
        log,
        scratch=[pltpu.VMEM((BLOCK, features), narrow)] * 2,
    )
    pieces = (early[0], late[0], early[1], early[2], late[1], late[2])
    (late,) = call(join_kernel, [ANY] * 2 + [VMEM] * 6, [some(128)], "join", 0, edge, log, *pieces)
    their_late = sent(late, 1)
    more = []
    if levels > 4:
        own = halve_rows(halve_rows(jnp.concatenate((keyval, inner), axis=1)))
        own = halve_rows(jnp.concatenate((own, side_2, jnp.concatenate(other_2)), axis=1))
        own = jnp.concatenate((own, late[:, :64], their_late[:, :64]), axis=1)
        own = jnp.concatenate((halve_rows(own), late[:, 64:], their_late[:, 64:]), axis=1)
        own = halve_rows(own)
        for level in range(5, levels + 1):
            more.append(sent(own, 1 << level - 1))
            own = halve_rows(jnp.concatenate((own, more[-1]), axis=1))
    mean, log = call(
        edge_kernel,
        [ANY, SMEM] + [VMEM] * 4,
        [wide, wide],
        "edge",
        0,
        late,
        position,
        queries,
        edge,
        mean,
        log,
    )
    far = [late, their_late, mean, log] + ups + more
    return call(
        far_kernel,
        [VMEM] * len(far),
        [up],
        "far",
        0,
        *far,
        scratch=[pltpu.VMEM(*up), pltpu.SemaphoreType.DMA((HEADS // GROUP,))],
        out_specs=[ANY],
    )[0]


def solution(mesh):
    return jax.shard_map(
        on_device,
        mesh=mesh,
        in_specs=(P(("streams", "seq"), None), P(None, ("streams", "seq"), None)),
        out_specs=P(("streams", "seq"), None),
        check_vma=False,
    )
```
